128 devices in a mesh: tok: 4 (over x), feat: 16 (over y_lo, z, core), row: 2 (over y_hi).
Axes of the slice: x: 4, y: 4 (y_hi: 2, y_lo: 2; y = y_hi * 2 + y_lo), z: 4, core: 2. Of those that a mesh axis runs over, the one named last changes fastest.
Arguments:
- quantized: bfloat16 [16384, 28672], P('tok', 'feat'), may hold values from -8 to 8
- exponents: int32 [16384, 224], P('tok', 'feat'), may hold values from -3 to 3
- weights: bfloat16 [8192, 28672], P(('tok', 'row'), 'feat'), may hold values from -6 to 6
- keep_mask: int32 [8192, 256], P(('tok', 'row')), may hold values from 0 to 1, as said below
Outputs:
- pruned: bfloat16 [8192, 28672], P(('tok', 'row'), 'feat')
The draws below stay inside these ranges and needn't reach their ends.
Inputs may be any that keep to these rules, and one draw needn't show every extreme that they name: `keep_mask`: in every row each group of four consecutive columns holds exactly two ones.
All inputs are finite; a program needn't handle non-finite values.
Results may differ from the reference program's by a relative error of at most 0.0012.
Values may be sent and summed in bfloat16 or wider, within the bound.
A program may use at most 128 MiB of HBM per device.

```python
import math
import jax
import jax.numpy as jnp
from jax import lax

ROWS = 8192
FF = 28672
PANEL = 256
QBLOCK = 128
TOKENS = 16384


def draw_keep_mask(key, part):
    scores = jax.random.randint(key, (ROWS, PANEL // 4, 4), 0, 1 << 20) * 4 + jnp.arange(4, dtype=jnp.int32)
    ranks = jnp.argsort(jnp.argsort(scores, axis=-1, stable=True), axis=-1, stable=True)
    return (ranks < 2).astype(jnp.int32).reshape(ROWS, PANEL)


def draw_quantized(key, part):
    shared_count = max(PANEL // 4, 2)
    noise_key = jax.random.fold_in(key, 101)
    token_key = jax.random.fold_in(key, 202)
    feature_key = jax.random.fold_in(key, 303)
    noise = jax.random.normal(noise_key, (TOKENS, FF), jnp.float32)
    token_factor = jax.random.normal(token_key, (TOKENS, shared_count), jnp.float32)
    feature_factor = jax.random.normal(feature_key, (shared_count, FF), jnp.float32) / math.sqrt(shared_count)
    common = jnp.dot(token_factor, feature_factor, precision=lax.Precision.HIGHEST)
    return jnp.clip(noise + common, -8.0, 8.0).astype(jnp.bfloat16)


def with_ends(drawn, key, low, high):
    spot = [jax.random.randint(jax.random.fold_in(key, axis), (), 0, length) for axis, length in enumerate(drawn.shape)]
    widest = drawn.shape.index(max(drawn.shape))
    neighbour = spot[:widest] + [(spot[widest] + 1) % drawn.shape[widest]] + spot[widest + 1:]
    return drawn.at[tuple(spot)].set(low).at[tuple(neighbour)].set(high)


def level_of(stream_key, shape, pieces, low, high):
    def one(position, parts):
        heights = jax.random.uniform(jax.random.fold_in(jax.random.fold_in(stream_key, 6), position), (parts,), jnp.float32, low / len(pieces), high / len(pieces))
        return jnp.repeat(jnp.exp(heights), shape[position] // parts).reshape((-1,) + (1,) * (len(shape) - position - 1))

    level = one(*pieces[0])
    for cut in pieces[1:]:
        level = level * one(*cut)
    return level


def bell_draw(stream_key, dims, deviation, limit, split=(), held_as=jnp.bfloat16):
    gain = level_of(stream_key, dims, split, -0.22, 0.18) if split else 1.0
    values = jax.random.normal(stream_key, dims, jnp.float32) * deviation * gain
    return jnp.minimum(jnp.maximum(values, -limit), limit).astype(held_as)


def setup_inputs(seed: int = 0) -> dict:
    arg_keys = jax.random.split(jax.random.key(seed), 5)
    quantized = draw_quantized(jax.random.fold_in(arg_keys[4], 71), 0)
    exponents = with_ends(jax.random.randint(arg_keys[1], (TOKENS, FF // QBLOCK), -3, 4), jax.random.fold_in(arg_keys[1], 1), -3, 3).astype(jnp.int32)
    weights = bell_draw(arg_keys[2], (ROWS, FF), 1.0, 6.0, ((0, 8), (1, 16)))
    keep_mask = draw_keep_mask(jax.random.fold_in(arg_keys[4], 71), 0)
    return dict(quantized=quantized, exponents=exponents, weights=weights, keep_mask=keep_mask)


def matmul_high(left, right):
    return jnp.dot(left, right, precision=lax.Precision.HIGHEST)

def factor_small(block):
    size = block.shape[0]
    lower = jnp.zeros_like(block)
    for j in range(size):
        head = lower[j, :j]
        diag_value = jnp.sqrt(block[j, j] - jnp.sum(head * head))
        column = (block[j:, j] - matmul_high(lower[j:, :j], head)) / diag_value
        lower = lower.at[j:, j].set(column)
    ident = jnp.eye(size, dtype=block.dtype)
    inverse = jnp.zeros_like(block)
    for i in range(size):
        row_value = (ident[i] - matmul_high(lower[i, :i], inverse[:i, :])) / lower[i, i]
        inverse = inverse.at[i].set(row_value)
    return (lower, inverse)

def factor_with_inverse(block):
    size = block.shape[0]
    if size <= 16:
        return factor_small(block)
    half = size // 2
    upper_lower, upper_inverse = factor_with_inverse(block[:half, :half])
    below = matmul_high(block[half:, :half], upper_inverse.T)
    rest = block[half:, half:] - matmul_high(below, below.T)
    rest_lower, rest_inverse = factor_with_inverse(rest)
    zeros_top = jnp.zeros((half, size - half), block.dtype)
    lower = jnp.concatenate([jnp.concatenate([upper_lower, zeros_top], axis=1), jnp.concatenate([below, rest_lower], axis=1)], axis=0)
    cross = -matmul_high(rest_inverse, matmul_high(below, upper_inverse))
    inverse = jnp.concatenate([jnp.concatenate([upper_inverse, zeros_top], axis=1), jnp.concatenate([cross, rest_inverse], axis=1)], axis=0)
    return (lower, inverse)

def reference(quantized, exponents, weights, keep_mask):
    tokens = quantized.shape[0]
    scales = jnp.exp2(exponents.astype(jnp.float32)).astype(jnp.bfloat16)
    activations = (quantized.reshape(tokens, FF // QBLOCK, QBLOCK) * scales[:, :, None]).reshape(tokens, FF)
    panel_acts = activations[:, :PANEL]
    hessian_panel = lax.dot_general(activations, panel_acts, (((0,), (0,)), ((), ())), preferred_element_type=jnp.float32)
    head_block = hessian_panel[:PANEL]
    damping = 0.01 * jnp.mean(jnp.diagonal(head_block))
    diag_block = head_block + damping * jnp.eye(PANEL, dtype=jnp.float32)
    factor, factor_inv = factor_with_inverse(diag_block)
    mask_float = keep_mask.astype(jnp.float32)
    pruned_error = weights[:, :PANEL].astype(jnp.float32) * (1.0 - mask_float)
    coefficients = matmul_high(matmul_high(pruned_error, factor_inv.T), factor_inv)
    update = jnp.dot(coefficients, hessian_panel.T, precision=lax.Precision.HIGHEST)
    columns = jnp.arange(FF)[None, :]
    masked = jnp.zeros((weights.shape[0], FF), jnp.float32).at[:, :PANEL].set(weights[:, :PANEL].astype(jnp.float32) * mask_float)
    result = jnp.where(columns < PANEL, masked, weights.astype(jnp.float32) + update)
    return result.astype(jnp.bfloat16)
```

```python
import functools

import jax
import jax.numpy as jnp
from jax import lax
from jax.experimental import pallas as pl
from jax.experimental.pallas import tpu as pltpu
from jax.sharding import PartitionSpec as P

PANEL = 256
QBLOCK = 128
CHUNK = 256
SQUARINGS = 18
POLISH = 2
MESH = pl.DeviceIdType.MESH
F32 = jnp.float32
BF16 = jnp.bfloat16


def high(left, right):
    return jnp.dot(left, right, precision=lax.Precision.HIGHEST, preferred_element_type=F32)


def split(value):
    top = value.astype(BF16)
    return top, (value - top.astype(F32)).astype(BF16)


def exchange_kernel(
    sizes,
    panel_ref, error_ref, quant_ref, scale_ref,
    hess_ref, inv_ref, error_out,
    acts, quant, part, summed, diag_part, diag, square, inverse, scaled,
    load_sem, quant_sem, arrive, send_z, send_y, send_c,
    diag_send, diag_recv, half_send, half_recv,
    err_send, err_recv,
    red_send, red_recv, all_send, all_recv, row_send, row_recv,
):
    n_chunks, n_pairs, n_err, width, n_feat, n_tok = sizes
    tok, feat, row = lax.axis_index("tok"), lax.axis_index("feat"), lax.axis_index("row")
    y_lo, z, core = feat // 8, (feat // 2) % 4, feat % 2
    strip = PANEL // n_tok
    n_quant = n_feat * width

    def at(t, y, zz, c, r):
        return (t, (y * 4 + zz) * 2 + c, r)

    z_up, z_down = (z + 1) % 4, (z + 3) % 4
    z_next = core * z_down + (1 - core) * z_up
    hops = core * ((4 - z) % 4) + (1 - core) * z
    cross_row = core * (1 - row) + (1 - core) * row
    to_z = at(tok, y_lo, z_next, core, row)
    to_y = at(tok, 1 - y_lo, z, core, cross_row)
    to_y_same = at(tok, 1 - y_lo, z, core, row)
    to_c = at(tok, y_lo, z, 1 - core, row)
    to_row = (tok, feat, 1 - row)
    peers = [((tok + k) % n_tok, feat, row) for k in range(1, n_tok)]
    greeted = [
        at(tok, y_lo, z_up, core, row), at(tok, y_lo, z_down, core, row),
        at(tok, 1 - y_lo, z, core, 0), at(tok, 1 - y_lo, z, core, 1),
        to_c, to_row,
    ] + peers
    even_y = y_lo == 0
    is_source = feat == 0
    is_twin = feat == 1
    can_z = jnp.logical_and(even_y, hops < 3)
    not_twin = feat != 1

    def own(j):
        return 2 * j + core

    def other(j):
        return 2 * j + 1 - core

    def rows_of(c, size=CHUNK):
        return pl.ds(pl.multiple_of(c * size, size), size)

    def load(c):
        return pltpu.make_async_copy(panel_ref.at[rows_of(c)], acts.at[rows_of(c)], arrive.at[c])

    def send(c, target, sem):
        return pltpu.make_async_remote_copy(
            src_ref=acts.at[rows_of(c)], dst_ref=acts.at[rows_of(c)], send_sem=sem.at[c],
            recv_sem=arrive.at[c], device_id=target, device_id_type=MESH)

    def quant_load(c):
        cols = pl.ds(pl.multiple_of(row * n_quant, 128), n_quant)
        return pltpu.make_async_copy(
            quant_ref.at[rows_of(c), cols], quant.at[rows_of(c)], quant_sem.at[c])

    @pl.when(is_source)
    def _():
        for c in range(n_chunks):
            load(c).start()
        pltpu.make_async_copy(error_ref, error_out, load_sem.at[0]).start()

    for c in range(n_chunks):
        quant_load(c).start()

    barrier = pltpu.get_barrier_semaphore()
    for device in greeted:
        pl.semaphore_signal(barrier, inc=1, device_id=device, device_id_type=MESH)
    pl.semaphore_wait(barrier, len(greeted))

    def forward(c):
        @pl.when(can_z)
        def _():
            send(c, to_z, send_z).start()

        @pl.when(even_y)
        def _():
            send(c, to_y, send_y).start()

        @pl.when(not_twin)
        def _():
            send(c, to_c, send_c).start()

    @pl.when(is_source)
    def _():
        def body(j, carry):
            load(own(j)).wait()
            forward(own(j))
            load(other(j)).wait()
            send(other(j), to_c, send_c).start()
            return carry

        lax.fori_loop(0, n_pairs, body, 0)

        def gram(c, carry):
            block = acts[rows_of(c), :]
            term = lax.dot_general(block, block, (((0,), (0,)), ((), ())), preferred_element_type=F32)

            @pl.when(c == 0)
            def _():
                diag_part[tok] = term

            @pl.when(c > 0)
            def _():
                diag_part[tok] += term

            return carry

        lax.fori_loop(0, n_chunks, gram, 0)
        for k, device in enumerate(peers):
            diag_copy(diag_part, diag_send, diag_recv, tok, k, device).start()

    def accumulate(c, first):
        quant_load(c).wait()
        scales = scale_ref[rows_of(c), :]
        blocks = []
        for b in range(n_quant // QBLOCK):
            scale = jnp.broadcast_to(scales[:, b:b + 1], (CHUNK, QBLOCK)).astype(BF16)
            blocks.append(quant[rows_of(c), b * QBLOCK:(b + 1) * QBLOCK] * scale)
        value = jnp.concatenate(blocks, axis=1)
        term = lax.dot_general(
            acts[rows_of(c), :], value, (((0,), (0,)), ((), ())), preferred_element_type=F32)
        for i in range(n_feat):
            piece = term[:, i * width:(i + 1) * width]
            if first:
                part[i] = piece
            else:
                part[i] += piece

    def pair(j, first):
        @pl.when(jnp.logical_not(is_source))
        def _():
            send(own(j), to_c, send_c).wait_recv()
            forward(own(j))

        accumulate(own(j), first)

        @pl.when(jnp.logical_not(is_source))
        def _():
            send(other(j), to_c, send_c).wait_recv()

        accumulate(other(j), False)

    pair(0, True)

    def later(j, carry):
        pair(j, False)
        return carry

    lax.fori_loop(1, n_pairs, later, 0)

    def red_copy(i, k, device):
        dest = device[0]
        return pltpu.make_async_remote_copy(
            src_ref=part.at[i, rows_of(dest, strip)], dst_ref=summed.at[i, tok],
            send_sem=red_send.at[i, k], recv_sem=red_recv.at[i, n_tok - 2 - k],
            device_id=device, device_id_type=MESH)

    for i in range(n_feat):
        for k, device in enumerate(peers):
            red_copy(i, k, device).start()

    def half_copy(h, target, slot):
        return pltpu.make_async_remote_copy(
            src_ref=diag.at[rows_of(h, PANEL // 2)], dst_ref=diag.at[rows_of(h, PANEL // 2)],
            send_sem=half_send.at[slot], recv_sem=half_recv.at[h],
            device_id=target, device_id_type=MESH)

    def err_copy(c, target, slot):
        return pltpu.make_async_remote_copy(
            src_ref=error_out.at[rows_of(c)], dst_ref=error_out.at[rows_of(c)],
            send_sem=err_send.at[slot, c], recv_sem=err_recv.at[c],
            device_id=target, device_id_type=MESH)

    def half_forward():
        @pl.when(can_z)
        def _():
            half_copy(core, to_z, 0).start()

        @pl.when(even_y)
        def _():
            half_copy(core, to_y, 1).start()

        @pl.when(not_twin)
        def _():
            half_copy(core, to_c, 2).start()

    def err_forward(c):
        @pl.when(can_z)
        def _():
            err_copy(c, to_z, 0).start()

        @pl.when(even_y)
        def _():
            err_copy(c, to_y_same, 1).start()

        @pl.when(not_twin)
        def _():
            err_copy(c, to_c, 2).start()

    @pl.when(is_source)
    def _():
        for k, device in enumerate(peers):
            diag_copy(diag_part, diag_send, diag_recv, tok, k, device).wait_recv()
        total = diag_part[0]
        for t in range(1, n_tok):
            total = total + diag_part[t]
        diag[...] = total
        half_forward()
        half_copy(1, to_c, 3).start()
        pltpu.make_async_copy(error_ref, error_out, load_sem.at[0]).wait()
        for j in range(n_err // 2):
            err_forward(own(j))
            err_copy(other(j), to_c, 2).start()

    @pl.when(jnp.logical_not(is_source))
    def _():
        half_copy(core, to_c, 0).wait_recv()
        half_forward()
        for j in range(n_err // 2):
            err_copy(own(j), to_c, 0).wait_recv()
            err_forward(own(j))
        half_copy(1 - core, to_c, 0).wait_recv()

    eye = (lax.broadcasted_iota(jnp.int32, (PANEL, PANEL), 0)
           == lax.broadcasted_iota(jnp.int32, (PANEL, PANEL), 1)).astype(F32)
    block = diag[...]
    trace = jnp.sum(jnp.sum(block * eye, axis=1, keepdims=True), axis=0, keepdims=True)
    damped = block + (0.01 / PANEL) * trace * eye
    shrink = 1.0 / (1.01 * trace)
    scaled[...] = damped * shrink
    square[...] = eye - scaled[...]
    inverse[...] = eye + square[...]

    def double(s, carry):
        r = square[...]
        r2 = high(r, r)
        square[...] = r2
        x = inverse[...]
        inverse[...] = x + high(x, r2)
        return carry

    lax.fori_loop(0, SQUARINGS, double, 0)

    def polish(s, carry):
        x = inverse[...]
        inverse[...] = x + high(x, eye - high(scaled[...], x))
        return carry

    lax.fori_loop(0, POLISH, polish, 0)
    inv_ref[...] = inverse[...] * shrink

    def all_copy(i, k, device):
        piece = hess_ref.at[row, i, rows_of(tok, strip)]
        return pltpu.make_async_remote_copy(
            src_ref=piece, dst_ref=piece, send_sem=all_send.at[i, k],
            recv_sem=all_recv.at[i, n_tok - 2 - k], device_id=device, device_id_type=MESH)

    def row_copy(i, k):
        owner = (tok + k) % n_tok
        piece = hess_ref.at[row, i, rows_of(owner, strip)]
        return pltpu.make_async_remote_copy(
            src_ref=piece, dst_ref=piece, send_sem=row_send.at[i, k],
            recv_sem=row_recv.at[i, k], device_id=to_row, device_id_type=MESH)

    for i in range(n_feat):
        for k, device in enumerate(peers):
            red_copy(i, k, device).wait_recv()
        mine = part[i, rows_of(tok, strip), :]
        for k in range(1, n_tok):
            mine = mine + summed[i, (tok + k) % n_tok]
        hess_ref[row, i, rows_of(tok, strip), :] = mine
        for k, device in enumerate(peers):
            all_copy(i, k, device).start()
        row_copy(i, 0).start()
    for i in range(n_feat):
        for k, device in enumerate(peers):
            all_copy(i, n_tok - 2 - k, device).wait_recv()
            row_copy(i, k + 1).start()

    for i in range(n_feat):
        for k in range(n_tok):
            row_copy(i, k).wait_recv()
    for i in range(n_feat):
        for k, device in enumerate(peers):
            red_copy(i, k, device).wait_send()
            all_copy(i, k, device).wait_send()
        for k in range(n_tok):
            row_copy(i, k).wait_send()

    @pl.when(jnp.logical_not(is_source))
    def _():
        for j in range(n_err // 2):
            err_copy(other(j), to_c, 0).wait_recv()

    def drain(j, carry):
        c = own(j)

        @pl.when(can_z)
        def _():
            send(c, to_z, send_z).wait_send()

        @pl.when(even_y)
        def _():
            send(c, to_y, send_y).wait_send()

        @pl.when(not_twin)
        def _():
            send(c, to_c, send_c).wait_send()

        @pl.when(is_source)
        def _():
            send(other(j), to_c, send_c).wait_send()

        return carry

    lax.fori_loop(0, n_pairs, drain, 0)

    @pl.when(can_z)
    def _():
        half_copy(core, to_z, 0).wait_send()
        for j in range(n_err // 2):
            err_copy(own(j), to_z, 0).wait_send()

    @pl.when(even_y)
    def _():
        half_copy(core, to_y, 1).wait_send()
        for j in range(n_err // 2):
            err_copy(own(j), to_y_same, 1).wait_send()

    @pl.when(not_twin)
    def _():
        half_copy(core, to_c, 2).wait_send()
        for j in range(n_err // 2):
            err_copy(own(j), to_c, 2).wait_send()

    @pl.when(is_source)
    def _():
        half_copy(1, to_c, 3).wait_send()
        for j in range(n_err // 2):
            err_copy(other(j), to_c, 2).wait_send()
        for k, device in enumerate(peers):
            diag_copy(diag_part, diag_send, diag_recv, tok, k, device).wait_send()


def diag_copy(diag_part, send_sem, recv_sem, tok, k, device):
    n = diag_part.shape[0]
    return pltpu.make_async_remote_copy(
        src_ref=diag_part.at[tok], dst_ref=diag_part.at[tok], send_sem=send_sem.at[k],
        recv_sem=recv_sem.at[n - 2 - k], device_id=device, device_id_type=MESH)


def exchange(panel, error, quantized, scales):
    tokens, columns = quantized.shape
    n_tok = lax.axis_size("tok")
    n_quant = columns // lax.axis_size("row")
    width = 128
    n_feat = n_quant // width
    n_chunks = tokens // CHUNK
    n_err = error.shape[0] // CHUNK
    strip = PANEL // n_tok
    sizes = (n_chunks, n_chunks // 2, n_err, width, n_feat, n_tok)
    dma = pltpu.SemaphoreType.DMA
    vmem = pl.BlockSpec(memory_space=pltpu.VMEM)
    hbm = pl.BlockSpec(memory_space=pl.ANY)
    return pl.pallas_call(
        functools.partial(exchange_kernel, sizes),
        out_shape=(
            jax.ShapeDtypeStruct((2, n_feat, PANEL, width), F32),
            jax.ShapeDtypeStruct((PANEL, PANEL), F32),
            jax.ShapeDtypeStruct(error.shape, BF16),
        ),
        in_specs=[hbm, hbm, hbm, vmem],
        out_specs=(vmem, vmem, vmem),
        scratch_shapes=[
            pltpu.VMEM((tokens, PANEL), BF16),
            pltpu.VMEM((tokens, n_quant), BF16),
            pltpu.VMEM((n_feat, PANEL, width), F32),
            pltpu.VMEM((n_feat, n_tok, strip, width), F32),
            pltpu.VMEM((n_tok, PANEL, PANEL), F32),
            pltpu.VMEM((PANEL, PANEL), F32),
            pltpu.VMEM((PANEL, PANEL), F32),
            pltpu.VMEM((PANEL, PANEL), F32),
            pltpu.VMEM((PANEL, PANEL), F32),
            dma((1,)), dma((n_chunks,)), dma((n_chunks,)),
            dma((n_chunks,)), dma((n_chunks,)), dma((n_chunks,)),
            dma((n_tok - 1,)), dma((n_tok - 1,)), dma((4,)), dma((2,)),
            dma((3, n_err)), dma((n_err,)),
            dma((n_feat, n_tok - 1)), dma((n_feat, n_tok - 1)),
            dma((n_feat, n_tok - 1)), dma((n_feat, n_tok - 1)),
            dma((n_feat, n_tok)), dma((n_feat, n_tok)),
        ],
        compiler_params=pltpu.CompilerParams(
            collective_id=0, has_side_effects=True, vmem_limit_bytes=60 * 1024 * 1024),
        name="exchange",
    )(panel, error, quantized, scales)


def update_kernel(feat_ref, hess_ref, inv_ref, error_ref, weights_ref, out_ref, product):
    n_rows, n_feat, _, width = hess_ref.shape

    @pl.when(pl.program_id(0) == 0)
    def _():
        top, low = split(inv_ref[...])
        for r in range(n_rows):
            for i in range(n_feat):
                h_top, h_low = split(hess_ref[r, i])
                value = (jnp.dot(top, h_top, preferred_element_type=F32)
                         + jnp.dot(top, h_low, preferred_element_type=F32)
                         + jnp.dot(low, h_top, preferred_element_type=F32))
                w_top, w_low = split(value)
                cols = pl.ds((r * n_feat + i) * width, width)
                product[:PANEL, cols] = w_top
                product[PANEL:, cols] = w_low

    error = error_ref[...]
    both = jnp.concatenate([error, error], axis=1)
    update = jnp.dot(both, product[...], preferred_element_type=F32)
    out_ref[...] = (weights_ref[...].astype(F32) + update).astype(BF16)

    @pl.when(feat_ref[0] == 0)
    def _():
        out_ref[:, :PANEL] = weights_ref[:, :PANEL] - error


def apply_update(feat, hess, inv, error, weights, tile=128):
    rows, columns = weights.shape
    return pl.pallas_call(
        update_kernel,
        grid=(rows // tile,),
        out_shape=jax.ShapeDtypeStruct(weights.shape, BF16),
        in_specs=[
            pl.BlockSpec(memory_space=pltpu.SMEM),
            pl.BlockSpec(memory_space=pltpu.VMEM),
            pl.BlockSpec(memory_space=pltpu.VMEM),
            pl.BlockSpec((tile, PANEL), lambda g: (g, 0)),
            pl.BlockSpec((tile, columns), lambda g: (g, 0)),
        ],
        out_specs=pl.BlockSpec((tile, columns), lambda g: (g, 0)),
        scratch_shapes=[pltpu.VMEM((2 * PANEL, columns), BF16)],
        name="update",
    )(feat, hess, inv, error, weights)


def shards(quantized, exponents, weights, keep_mask):
    tokens = quantized.shape[0]
    blocks = exponents.shape[1]
    scales = jnp.exp2(exponents.astype(F32))
    own = PANEL // QBLOCK
    panel = (
        quantized[:, :PANEL].reshape(tokens, own, QBLOCK)
        * scales[:, :own].astype(BF16)[:, :, None]
    ).reshape(tokens, PANEL)
    half = blocks // lax.axis_size("row")
    row_scales = lax.dynamic_slice_in_dim(scales, lax.axis_index("row") * half, half, 1)
    error = jnp.where(keep_mask == 0, weights[:, :PANEL], jnp.zeros((), BF16))
    hess, inv, error = exchange(panel, error, quantized, row_scales)
    feat = lax.axis_index("feat").astype(jnp.int32).reshape(1)
    return apply_update(feat, hess, inv, error, weights)


def solution(mesh):
    placed = (
        P("tok", "feat"),
        P("tok", "feat"),
        P(("tok", "row"), "feat"),
        P(("tok", "row"), None),
    )
    return jax.shard_map(
        shards, mesh=mesh, in_specs=placed, out_specs=P(("tok", "row"), "feat"), check_vma=False
    )
```

```python
import functools

import jax
import jax.numpy as jnp
from jax import lax
from jax.experimental import pallas as pl
from jax.experimental.pallas import tpu as pltpu
from jax.sharding import PartitionSpec as P

PANEL = 256
QBLOCK = 128
CHUNK = 256
LAG = 4
SQUARINGS = 18
POLISH = 2
MESH = pl.DeviceIdType.MESH
F32 = jnp.float32
BF16 = jnp.bfloat16


def high(left, right):
    return jnp.dot(left, right, precision=lax.Precision.HIGHEST, preferred_element_type=F32)


def three(left, right):
    l_top, l_low = split(left)
    r_top, r_low = split(right)
    return (jnp.dot(l_top, r_top, preferred_element_type=F32)
            + jnp.dot(l_top, r_low, preferred_element_type=F32)
            + jnp.dot(l_low, r_top, preferred_element_type=F32))


def split(value):
    top = value.astype(BF16)
    return top, (value - top.astype(F32)).astype(BF16)


def exchange_kernel(
    sizes,
    quant_ref, exps_hbm, weights_ref, keep_ref,
    product_ref, error_out,
    exps_ref, raw, acts, quant, weights, keep, hess_ref, part, summed, diag_part, diag, square, inverse, scaled,
    load_sem, quant_sem, arrive, send_z, send_y, send_c,
    diag_send, diag_recv, half_send, half_recv,
    err_send, err_recv,
    red_send, red_recv, all_send, all_recv, row_send, row_recv,
):
    n_chunks, n_pairs, n_err, width, n_feat, n_tok = sizes
    tok, feat, row = lax.axis_index("tok"), lax.axis_index("feat"), lax.axis_index("row")
    y_lo, z, core = feat // 8, (feat // 2) % 4, feat % 2
    strip = PANEL // n_tok
    n_quant = n_feat * width

    def at(t, y, zz, c, r):
        return (t, (y * 4 + zz) * 2 + c, r)

    z_up, z_down = (z + 1) % 4, (z + 3) % 4
    z_next = core * z_down + (1 - core) * z_up
    hops = core * ((4 - z) % 4) + (1 - core) * z
    cross_row = core * (1 - row) + (1 - core) * row
    to_z = at(tok, y_lo, z_next, core, row)
    to_y = at(tok, 1 - y_lo, z, core, cross_row)
    to_y_same = at(tok, 1 - y_lo, z, core, row)
    to_c = at(tok, y_lo, z, 1 - core, row)
    to_row = (tok, feat, 1 - row)
    peers = [((tok + k) % n_tok, feat, row) for k in range(1, n_tok)]
    greeted = [
        at(tok, y_lo, z_up, core, row), at(tok, y_lo, z_down, core, row),
        at(tok, 1 - y_lo, z, core, 0), at(tok, 1 - y_lo, z, core, 1),
        to_c, to_row,
    ] + peers
    even_y = y_lo == 0
    is_source = feat == 0
    is_twin = feat == 1
    can_z = jnp.logical_and(even_y, hops < 3)
    not_twin = feat != 1

    def own(j):
        return 2 * j + core

    def other(j):
        return 2 * j + 1 - core

    def rows_of(c, size=CHUNK):
        return pl.ds(pl.multiple_of(c * size, size), size)

    def load(c):
        return pltpu.make_async_copy(
            quant_ref.at[rows_of(c), pl.ds(0, PANEL)], raw.at[rows_of(c)], arrive.at[c])

    def error_load():
        return (pltpu.make_async_copy(weights_ref.at[:, pl.ds(0, PANEL)], weights, load_sem.at[0]),
                pltpu.make_async_copy(keep_ref, keep, load_sem.at[1]))

    def scales_of(c):
        exps = exps_ref[:, rows_of(c)].astype(F32)
        return jnp.exp2(exps).T

    def spread(column):
        return jnp.broadcast_to(column, (CHUNK, QBLOCK)).astype(BF16)

    def send(c, target, sem):
        return pltpu.make_async_remote_copy(
            src_ref=acts.at[rows_of(c)], dst_ref=acts.at[rows_of(c)], send_sem=sem.at[c],
            recv_sem=arrive.at[c], device_id=target, device_id_type=MESH)

    def quant_load(c):
        cols = pl.ds(pl.multiple_of(row * n_quant, 128), n_quant)
        return pltpu.make_async_copy(
            quant_ref.at[rows_of(c), cols], quant.at[rows_of(c)], quant_sem.at[c])

    exps_copy = pltpu.make_async_copy(exps_hbm, exps_ref, load_sem.at[2])
    exps_copy.start()

    @pl.when(is_source)
    def _():
        for c in range(n_chunks):
            load(c).start()
        for copy in error_load():
            copy.start()

    for c in range(n_chunks):
        quant_load(c).start()

    barrier = pltpu.get_barrier_semaphore()
    for device in greeted:
        pl.semaphore_signal(barrier, inc=1, device_id=device, device_id_type=MESH)
    pl.semaphore_wait(barrier, len(greeted))
    exps_copy.wait()

    def forward(c):
        @pl.when(can_z)
        def _():
            send(c, to_z, send_z).start()

        @pl.when(even_y)
        def _():
            send(c, to_y, send_y).start()

        @pl.when(not_twin)
        def _():
            send(c, to_c, send_c).start()

    @pl.when(is_source)
    def _():
        def scale(c):
            load(c).wait()
            scales = scales_of(c)
            for b in range(PANEL // QBLOCK):
                cols = slice(b * QBLOCK, (b + 1) * QBLOCK)
                acts[rows_of(c), cols] = raw[rows_of(c), cols] * spread(scales[:, b:b + 1])

        def pass_on(j):
            forward(own(j))
            send(other(j), to_c, send_c).start()

        def body(j, carry):
            scale(own(j))
            scale(other(j))
            pass_on(j - 1)
            return carry

        scale(0)
        scale(1)
        lax.fori_loop(1, n_pairs, body, 0)
        pass_on(n_pairs - 1)

        def gram(c, carry):
            block = acts[rows_of(c), :]
            term = lax.dot_general(block, block, (((0,), (0,)), ((), ())), preferred_element_type=F32)

            @pl.when(c == 0)
            def _():
                diag_part[tok] = term

            @pl.when(c > 0)
            def _():
                diag_part[tok] += term

            return carry

        lax.fori_loop(0, n_chunks, gram, 0)
        for k, device in enumerate(peers):
            diag_copy(diag_part, diag_send, diag_recv, tok, k, device).start()

    def accumulate(c, first):
        quant_load(c).wait()
        scales = scales_of(c)
        blocks = []
        n_blocks = n_quant // QBLOCK
        for b in range(n_blocks):
            column = jnp.where(row == 0, scales[:, b:b + 1], scales[:, n_blocks + b:n_blocks + b + 1])
            blocks.append(quant[rows_of(c), b * QBLOCK:(b + 1) * QBLOCK] * spread(column))
        value = jnp.concatenate(blocks, axis=1)
        term = lax.dot_general(
            acts[rows_of(c), :], value, (((0,), (0,)), ((), ())), preferred_element_type=F32)
        for i in range(n_feat):
            piece = term[:, i * width:(i + 1) * width]
            if first:
                part[i] = piece
            else:
                part[i] += piece

    def own_step(j, first):
        @pl.when(jnp.logical_not(is_source))
        def _():
            send(own(j), to_c, send_c).wait_recv()
            forward(own(j))

        accumulate(own(j), first)

    def other_step(j):
        @pl.when(jnp.logical_not(is_source))
        def _():
            send(other(j), to_c, send_c).wait_recv()

        accumulate(other(j), False)

    def only_own(j, carry):
        own_step(j, False)
        return carry

    def both(j, carry):
        own_step(j, False)
        other_step(j - LAG)
        return carry

    def only_other(j, carry):
        other_step(j)
        return carry

    own_step(0, True)
    lax.fori_loop(1, LAG, only_own, 0)
    lax.fori_loop(LAG, n_pairs, both, 0)
    lax.fori_loop(n_pairs - LAG, n_pairs, only_other, 0)

    def red_copy(i, k, device):
        dest = device[0]
        return pltpu.make_async_remote_copy(
            src_ref=part.at[i, rows_of(dest, strip)], dst_ref=summed.at[i, tok],
            send_sem=red_send.at[i, k], recv_sem=red_recv.at[i, n_tok - 2 - k],
            device_id=device, device_id_type=MESH)

    for i in range(n_feat):
        for k, device in enumerate(peers):
            red_copy(i, k, device).start()

    def half_copy(h, target, slot):
        return pltpu.make_async_remote_copy(
            src_ref=diag.at[rows_of(h, PANEL // 2)], dst_ref=diag.at[rows_of(h, PANEL // 2)],
            send_sem=half_send.at[slot], recv_sem=half_recv.at[h],
            device_id=target, device_id_type=MESH)

    def err_copy(c, target, slot):
        return pltpu.make_async_remote_copy(
            src_ref=error_out.at[rows_of(c)], dst_ref=error_out.at[rows_of(c)],
            send_sem=err_send.at[slot, c], recv_sem=err_recv.at[c],
            device_id=target, device_id_type=MESH)

    def half_forward():
        @pl.when(can_z)
        def _():
            half_copy(core, to_z, 0).start()

        @pl.when(even_y)
        def _():
            half_copy(core, to_y, 1).start()

        @pl.when(not_twin)
        def _():
            half_copy(core, to_c, 2).start()

    def err_forward(c):
        @pl.when(can_z)
        def _():
            err_copy(c, to_z, 0).start()

        @pl.when(even_y)
        def _():
            err_copy(c, to_y_same, 1).start()

        @pl.when(not_twin)
        def _():
            err_copy(c, to_c, 2).start()

    @pl.when(is_source)
    def _():
        for copy in error_load():
            copy.wait()
        error_out[...] = jnp.where(keep[...] == 0, weights[...].astype(F32), 0.0).astype(BF16)
        for k, device in enumerate(peers):
            diag_copy(diag_part, diag_send, diag_recv, tok, k, device).wait_recv()
        total = diag_part[0]
        for t in range(1, n_tok):
            total = total + diag_part[t]
        diag[...] = total
        half_forward()
        half_copy(1, to_c, 3).start()
        for j in range(n_err // 2):
            err_forward(own(j))
            err_copy(other(j), to_c, 2).start()

    def all_copy(i, k, device):
        piece = hess_ref.at[row, i, rows_of(tok, strip)]
        return pltpu.make_async_remote_copy(
            src_ref=piece, dst_ref=piece, send_sem=all_send.at[i, k],
            recv_sem=all_recv.at[i, n_tok - 2 - k], device_id=device, device_id_type=MESH)

    def row_copy(i, k):
        owner = (tok + k) % n_tok
        piece = hess_ref.at[row, i, rows_of(owner, strip)]
        return pltpu.make_async_remote_copy(
            src_ref=piece, dst_ref=piece, send_sem=row_send.at[i, k],
            recv_sem=row_recv.at[i, k], device_id=to_row, device_id_type=MESH)

    for i in range(n_feat):
        for k, device in enumerate(peers):
            red_copy(i, k, device).wait_recv()
        mine = part[i, rows_of(tok, strip), :]
        for k in range(1, n_tok):
            mine = mine + summed[i, (tok + k) % n_tok]
        hess_ref[row, i, rows_of(tok, strip), :] = mine
        for k, device in enumerate(peers):
            all_copy(i, k, device).start()
        row_copy(i, 0).start()

    @pl.when(jnp.logical_not(is_source))
    def _():
        half_copy(core, to_c, 0).wait_recv()
        half_forward()
        for j in range(n_err // 2):
            err_copy(own(j), to_c, 0).wait_recv()
            err_forward(own(j))
        half_copy(1 - core, to_c, 0).wait_recv()

    eye = (lax.broadcasted_iota(jnp.int32, (PANEL, PANEL), 0)
           == lax.broadcasted_iota(jnp.int32, (PANEL, PANEL), 1)).astype(F32)
    block = diag[...]
    trace = jnp.sum(jnp.sum(block * eye, axis=1, keepdims=True), axis=0, keepdims=True)
    shrink = 1.0 / (1.01 * trace)
    scaled[...] = (block + (0.01 / PANEL) * trace * eye) * shrink
    square[...] = eye - scaled[...]
    inverse[...] = eye + square[...]

    def double(_, carry):
        r = square[...]
        r2 = three(r, r)
        square[...] = r2
        x = inverse[...]
        inverse[...] = x + three(x, r2)
        return carry

    steps = -(-SQUARINGS // (n_feat - 1))
    for i in range(n_feat):
        lax.fori_loop(0, steps if i else SQUARINGS - steps * (n_feat - 1), double, 0)
        for k, device in enumerate(peers):
            all_copy(i, n_tok - 2 - k, device).wait_recv()
            row_copy(i, k + 1).start()

    def polish(_, carry):
        x = inverse[...]
        inverse[...] = x + high(eye - high(x, scaled[...]), x)
        return carry

    lax.fori_loop(0, POLISH, polish, 0)
    top, low = split(inverse[...] * shrink)

    def multiply(r, i):
        h_top, h_low = split(hess_ref[r, i])
        w_top, w_low = split(
            jnp.dot(top, h_top, preferred_element_type=F32)
            + jnp.dot(top, h_low, preferred_element_type=F32)
            + jnp.dot(low, h_top, preferred_element_type=F32))
        cols = pl.ds(pl.multiple_of((r * n_feat + i) * width, width), width)
        product_ref[:PANEL, cols] = w_top
        product_ref[PANEL:, cols] = w_low

    for i in range(n_feat):
        multiply(row, i)
    for i in range(n_feat):
        for k in range(n_tok):
            row_copy(i, k).wait_recv()
        multiply(1 - row, i)

    for i in range(n_feat):
        for k, device in enumerate(peers):
            red_copy(i, k, device).wait_send()
            all_copy(i, k, device).wait_send()
        for k in range(n_tok):
            row_copy(i, k).wait_send()

    @pl.when(jnp.logical_not(is_source))
    def _():
        for j in range(n_err // 2):
            err_copy(other(j), to_c, 0).wait_recv()

    def drain(j, carry):
        c = own(j)

        @pl.when(can_z)
        def _():
            send(c, to_z, send_z).wait_send()

        @pl.when(even_y)
        def _():
            send(c, to_y, send_y).wait_send()

        @pl.when(not_twin)
        def _():
            send(c, to_c, send_c).wait_send()

        @pl.when(is_source)
        def _():
            send(other(j), to_c, send_c).wait_send()

        return carry

    lax.fori_loop(0, n_pairs, drain, 0)

    @pl.when(can_z)
    def _():
        half_copy(core, to_z, 0).wait_send()
        for j in range(n_err // 2):
            err_copy(own(j), to_z, 0).wait_send()

    @pl.when(even_y)
    def _():
        half_copy(core, to_y, 1).wait_send()
        for j in range(n_err // 2):
            err_copy(own(j), to_y_same, 1).wait_send()

    @pl.when(not_twin)
    def _():
        half_copy(core, to_c, 2).wait_send()
        for j in range(n_err // 2):
            err_copy(own(j), to_c, 2).wait_send()

    @pl.when(is_source)
    def _():
        half_copy(1, to_c, 3).wait_send()
        for j in range(n_err // 2):
            err_copy(other(j), to_c, 2).wait_send()
        for k, device in enumerate(peers):
            diag_copy(diag_part, diag_send, diag_recv, tok, k, device).wait_send()


def diag_copy(diag_part, send_sem, recv_sem, tok, k, device):
    n = diag_part.shape[0]
    return pltpu.make_async_remote_copy(
        src_ref=diag_part.at[tok], dst_ref=diag_part.at[tok], send_sem=send_sem.at[k],
        recv_sem=recv_sem.at[n - 2 - k], device_id=device, device_id_type=MESH)


def exchange(quantized, exponents, weights, keep_mask):
    tokens, columns = quantized.shape
    rows = weights.shape[0]
    n_tok = lax.axis_size("tok")
    n_quant = columns // lax.axis_size("row")
    width = 128
    n_feat = n_quant // width
    n_chunks = tokens // CHUNK
    n_err = rows // CHUNK
    strip = PANEL // n_tok
    sizes = (n_chunks, n_chunks // 2, n_err, width, n_feat, n_tok)
    dma = pltpu.SemaphoreType.DMA
    vmem = pl.BlockSpec(memory_space=pltpu.VMEM)
    hbm = pl.BlockSpec(memory_space=pltpu.HBM)
    return pl.pallas_call(
        functools.partial(exchange_kernel, sizes),
        out_shape=(
            jax.ShapeDtypeStruct((2 * PANEL, columns), BF16),
            jax.ShapeDtypeStruct((rows, PANEL), BF16),
        ),
        in_specs=[hbm, hbm, hbm, hbm],
        out_specs=(vmem, vmem),
        scratch_shapes=[
            pltpu.VMEM(exponents.T.shape, jnp.int32),
            pltpu.VMEM((tokens, PANEL), BF16),
            pltpu.VMEM((tokens, PANEL), BF16),
            pltpu.VMEM((tokens, n_quant), BF16),
            pltpu.VMEM((rows, PANEL), BF16),
            pltpu.VMEM((rows, PANEL), jnp.int32),
            pltpu.VMEM((2, n_feat, PANEL, width), F32),
            pltpu.VMEM((n_feat, PANEL, width), F32),
            pltpu.VMEM((n_feat, n_tok, strip, width), F32),
            pltpu.VMEM((n_tok, PANEL, PANEL), F32),
            pltpu.VMEM((PANEL, PANEL), F32),
            pltpu.VMEM((PANEL, PANEL), F32),
            pltpu.VMEM((PANEL, PANEL), F32),
            pltpu.VMEM((PANEL, PANEL), F32),
            dma((3,)), dma((n_chunks,)), dma((n_chunks,)),
            dma((n_chunks,)), dma((n_chunks,)), dma((n_chunks,)),
            dma((n_tok - 1,)), dma((n_tok - 1,)), dma((4,)), dma((2,)),
            dma((3, n_err)), dma((n_err,)),
            dma((n_feat, n_tok - 1)), dma((n_feat, n_tok - 1)),
            dma((n_feat, n_tok - 1)), dma((n_feat, n_tok - 1)),
            dma((n_feat, n_tok)), dma((n_feat, n_tok)),
        ],
        compiler_params=pltpu.CompilerParams(
            collective_id=0, has_side_effects=True, vmem_limit_bytes=32 * 1024 * 1024),
        name="exchange",
    )(*[pltpu.with_memory_space_constraint(x, pltpu.HBM)
        for x in (quantized, exponents.T, weights, keep_mask)])


def update_kernel(feat_ref, product_ref, error_ref, weights_ref, out_ref):
    error = error_ref[...]
    both = jnp.concatenate([error, error], axis=1)
    update = jnp.dot(both, product_ref[...], preferred_element_type=F32)
    out_ref[...] = (weights_ref[...].astype(F32) + update).astype(BF16)

    @pl.when(feat_ref[0] == 0)
    def _():
        out_ref[:, :PANEL] = weights_ref[:, :PANEL] - error


def apply_update(feat, product, error, weights, tile=128):
    rows, columns = weights.shape
    return pl.pallas_call(
        update_kernel,
        grid=(rows // tile,),
        out_shape=jax.ShapeDtypeStruct(weights.shape, BF16),
        in_specs=[
            pl.BlockSpec(memory_space=pltpu.SMEM),
            pl.BlockSpec(memory_space=pltpu.VMEM),
            pl.BlockSpec((tile, PANEL), lambda g: (g, 0)),
            pl.BlockSpec((tile, columns), lambda g: (g, 0)),
        ],
        out_specs=pl.BlockSpec((tile, columns), lambda g: (g, 0)),
        compiler_params=pltpu.CompilerParams(vmem_limit_bytes=24 * 1024 * 1024),
        name="update",
    )(feat, product, error, weights)


def shards(quantized, exponents, weights, keep_mask):
    product, error = exchange(quantized, exponents, weights, keep_mask)
    feat = lax.axis_index("feat").astype(jnp.int32).reshape(1)
    return apply_update(feat, product, error, weights)


def solution(mesh):
    placed = (
        P("tok", "feat"),
        P("tok", "feat"),
        P(("tok", "row"), "feat"),
        P(("tok", "row"), None),
    )
    return jax.shard_map(
        shards, mesh=mesh, in_specs=placed, out_specs=P(("tok", "row"), "feat"), check_vma=False
    )
```

```python
import functools

import jax
import jax.numpy as jnp
from jax import lax
from jax.experimental import pallas as pl
from jax.experimental.pallas import tpu as pltpu
from jax.sharding import PartitionSpec as P

PANEL = 256
QBLOCK = 128
CHUNK = 256
LAG = 6
SQUARINGS = 18
POLISH = 2
MESH = pl.DeviceIdType.MESH
F32 = jnp.float32
BF16 = jnp.bfloat16


def high(left, right):
    return jnp.dot(left, right, precision=lax.Precision.HIGHEST, preferred_element_type=F32)


def three(left, right):
    l_top, l_low = split(left)
    r_top, r_low = split(right)
    return (jnp.dot(l_top, r_top, preferred_element_type=F32)
            + jnp.dot(l_top, r_low, preferred_element_type=F32)
            + jnp.dot(l_low, r_top, preferred_element_type=F32))


def split(value):
    top = value.astype(BF16)
    return top, (value - top.astype(F32)).astype(BF16)


def exchange_kernel(
    sizes,
    quant_ref, exps_hbm, weights_ref, keep_ref,
    product_ref, error_out,
    exps_ref, raw, acts, quant, weights, keep, hess_ref, part, summed, diag_part, diag, square, inverse, scaled,
    load_sem, quant_sem, arrive, send_z, send_y, send_c,
    diag_send, diag_recv, half_send, half_recv,
    err_send, err_recv,
    red_send, red_recv, all_send, all_recv, row_send, row_recv,
):
    n_chunks, n_pairs, n_err, width, n_feat, n_tok = sizes
    tok, feat, row = lax.axis_index("tok"), lax.axis_index("feat"), lax.axis_index("row")
    y_lo, z, core = feat // 8, (feat // 2) % 4, feat % 2
    strip = PANEL // n_tok
    n_quant = n_feat * width

    def at(t, y, zz, c, r):
        return (t, (y * 4 + zz) * 2 + c, r)

    z_up, z_down = (z + 1) % 4, (z + 3) % 4
    z_next = core * z_down + (1 - core) * z_up
    hops = core * ((4 - z) % 4) + (1 - core) * z
    cross_row = core * (1 - row) + (1 - core) * row
    to_z = at(tok, y_lo, z_next, core, row)
    to_y = at(tok, 1 - y_lo, z, core, cross_row)
    to_y_same = at(tok, 1 - y_lo, z, core, row)
    to_c = at(tok, y_lo, z, 1 - core, row)
    to_row = (tok, feat, 1 - row)
    peers = [((tok + k) % n_tok, feat, row) for k in range(1, n_tok)]
    greeted = [
        at(tok, y_lo, z_up, core, row), at(tok, y_lo, z_down, core, row),
        at(tok, 1 - y_lo, z, core, 0), at(tok, 1 - y_lo, z, core, 1),
        to_c, to_row,
    ] + peers
    even_y = y_lo == 0
    is_source = feat == 0
    is_twin = feat == 1
    can_z = jnp.logical_and(even_y, hops < 3)
    not_twin = feat != 1
    chain_z = hops < 3
    root_y = jnp.logical_and(even_y, z == 0)

    def own(j):
        return 2 * j + core

    def other(j):
        return 2 * j + 1 - core

    def rows_of(c, size=CHUNK):
        return pl.ds(pl.multiple_of(c * size, size), size)

    def load(c):
        return pltpu.make_async_copy(
            quant_ref.at[rows_of(c), pl.ds(0, PANEL)], raw.at[rows_of(c)], arrive.at[c])

    def error_load():
        return (pltpu.make_async_copy(weights_ref.at[:, pl.ds(0, PANEL)], weights, load_sem.at[0]),
                pltpu.make_async_copy(keep_ref, keep, load_sem.at[1]))

    def scales_of(c):
        exps = exps_ref[:, rows_of(c)].astype(F32)
        return jnp.exp2(exps).T

    def spread(column):
        return jnp.broadcast_to(column, (CHUNK, QBLOCK)).astype(BF16)

    def send(c, target, sem):
        return pltpu.make_async_remote_copy(
            src_ref=acts.at[rows_of(c)], dst_ref=acts.at[rows_of(c)], send_sem=sem.at[c],
            recv_sem=arrive.at[c], device_id=target, device_id_type=MESH)

    def quant_load(c):
        cols = pl.ds(pl.multiple_of(row * n_quant, 128), n_quant)
        return pltpu.make_async_copy(
            quant_ref.at[rows_of(c), cols], quant.at[rows_of(c)], quant_sem.at[c])

    exps_copy = pltpu.make_async_copy(exps_hbm, exps_ref, load_sem.at[2])
    exps_copy.start()

    @pl.when(is_source)
    def _():
        for c in range(n_chunks):
            load(c).start()
        for copy in error_load():
            copy.start()

    for c in range(n_chunks):
        quant_load(c).start()

    barrier = pltpu.get_barrier_semaphore()
    for device in greeted:
        pl.semaphore_signal(barrier, inc=1, device_id=device, device_id_type=MESH)
    pl.semaphore_wait(barrier, len(greeted))
    exps_copy.wait()

    def forward(c):
        @pl.when(can_z)
        def _():
            send(c, to_z, send_z).start()

        @pl.when(even_y)
        def _():
            send(c, to_y, send_y).start()

        @pl.when(not_twin)
        def _():
            send(c, to_c, send_c).start()

    @pl.when(is_source)
    def _():
        def scale(c):
            load(c).wait()
            scales = scales_of(c)
            for b in range(PANEL // QBLOCK):
                cols = slice(b * QBLOCK, (b + 1) * QBLOCK)
                acts[rows_of(c), cols] = raw[rows_of(c), cols] * spread(scales[:, b:b + 1])

        def pass_on(j):
            forward(own(j))
            send(other(j), to_c, send_c).start()

        def body(j, carry):
            scale(own(j))
            scale(other(j))
            pass_on(j - 1)
            return carry

        scale(0)
        scale(1)
        lax.fori_loop(1, n_pairs, body, 0)
        pass_on(n_pairs - 1)

        def gram(c, carry):
            block = acts[rows_of(c), :]
            term = lax.dot_general(block, block, (((0,), (0,)), ((), ())), preferred_element_type=F32)

            @pl.when(c == 0)
            def _():
                diag_part[tok] = term

            @pl.when(c > 0)
            def _():
                diag_part[tok] += term

            return carry

        lax.fori_loop(0, n_chunks, gram, 0)
        for k, device in enumerate(peers):
            diag_copy(diag_part, diag_send, diag_recv, tok, k, device).start()

    def accumulate(c, first):
        quant_load(c).wait()
        scales = scales_of(c)
        blocks = []
        n_blocks = n_quant // QBLOCK
        for b in range(n_blocks):
            column = jnp.where(row == 0, scales[:, b:b + 1], scales[:, n_blocks + b:n_blocks + b + 1])
            blocks.append(quant[rows_of(c), b * QBLOCK:(b + 1) * QBLOCK] * spread(column))
        value = jnp.concatenate(blocks, axis=1)
        term = lax.dot_general(
            acts[rows_of(c), :], value, (((0,), (0,)), ((), ())), preferred_element_type=F32)
        for i in range(n_feat):
            piece = term[:, i * width:(i + 1) * width]
            if first:
                part[i] = piece
            else:
                part[i] += piece

    def own_step(j, first):
        @pl.when(jnp.logical_not(is_source))
        def _():
            send(own(j), to_c, send_c).wait_recv()
            forward(own(j))

        accumulate(own(j), first)

    def other_step(j):
        @pl.when(jnp.logical_not(is_source))
        def _():
            send(other(j), to_c, send_c).wait_recv()

        accumulate(other(j), False)

    def only_own(j, carry):
        own_step(j, False)
        return carry

    def both(j, carry):
        own_step(j, False)
        other_step(j - LAG)
        return carry

    def only_other(j, carry):
        other_step(j)
        return carry

    own_step(0, True)
    lax.fori_loop(1, LAG, only_own, 0)
    lax.fori_loop(LAG, n_pairs, both, 0)
    lax.fori_loop(n_pairs - LAG, n_pairs, only_other, 0)

    def red_copy(i, k, device):
        dest = device[0]
        return pltpu.make_async_remote_copy(
            src_ref=part.at[i, rows_of(dest, strip)], dst_ref=summed.at[i, tok],
            send_sem=red_send.at[i, k], recv_sem=red_recv.at[i, n_tok - 2 - k],
            device_id=device, device_id_type=MESH)

    for i in range(n_feat):
        for k, device in enumerate(peers):
            red_copy(i, k, device).start()

    def half_copy(h, target, slot):
        return pltpu.make_async_remote_copy(
            src_ref=diag.at[rows_of(h, PANEL // 2)], dst_ref=diag.at[rows_of(h, PANEL // 2)],
            send_sem=half_send.at[slot], recv_sem=half_recv.at[h],
            device_id=target, device_id_type=MESH)

    def err_copy(c, target, slot):
        return pltpu.make_async_remote_copy(
            src_ref=error_out.at[rows_of(c)], dst_ref=error_out.at[rows_of(c)],
            send_sem=err_send.at[slot, c], recv_sem=err_recv.at[c],
            device_id=target, device_id_type=MESH)

    def half_forward():
        @pl.when(chain_z)
        def _():
            half_copy(core, to_z, 0).start()

        @pl.when(root_y)
        def _():
            half_copy(core, to_y, 1).start()

        @pl.when(not_twin)
        def _():
            half_copy(core, to_c, 2).start()

    def err_forward(c):
        @pl.when(chain_z)
        def _():
            err_copy(c, to_z, 0).start()

        @pl.when(root_y)
        def _():
            err_copy(c, to_y_same, 1).start()

        @pl.when(not_twin)
        def _():
            err_copy(c, to_c, 2).start()

    @pl.when(is_source)
    def _():
        for copy in error_load():
            copy.wait()
        error_out[...] = jnp.where(keep[...] == 0, weights[...].astype(F32), 0.0).astype(BF16)
        for k, device in enumerate(peers):
            diag_copy(diag_part, diag_send, diag_recv, tok, k, device).wait_recv()
        total = diag_part[0]
        for t in range(1, n_tok):
            total = total + diag_part[t]
        diag[...] = total
        half_forward()
        half_copy(1, to_c, 3).start()
        for j in range(n_err // 2):
            err_forward(own(j))
            err_copy(other(j), to_c, 2).start()

    @pl.when(jnp.logical_not(is_source))
    def _():
        half_copy(core, to_c, 0).wait_recv()
        half_forward()
        half_copy(1 - core, to_c, 0).wait_recv()

    def all_copy(i, k, device):
        piece = hess_ref.at[row, i, rows_of(tok, strip)]
        return pltpu.make_async_remote_copy(
            src_ref=piece, dst_ref=piece, send_sem=all_send.at[i, k],
            recv_sem=all_recv.at[i, n_tok - 2 - k], device_id=device, device_id_type=MESH)

    def row_copy(i, k):
        owner = (tok + k) % n_tok
        piece = hess_ref.at[row, i, rows_of(owner, strip)]
        return pltpu.make_async_remote_copy(
            src_ref=piece, dst_ref=piece, send_sem=row_send.at[i, k],
            recv_sem=row_recv.at[i, k], device_id=to_row, device_id_type=MESH)

    for i in range(n_feat):
        for k, device in enumerate(peers):
            red_copy(i, k, device).wait_recv()
        mine = part[i, rows_of(tok, strip), :]
        for k in range(1, n_tok):
            mine = mine + summed[i, (tok + k) % n_tok]
        hess_ref[row, i, rows_of(tok, strip), :] = mine
        for k, device in enumerate(peers):
            all_copy(i, k, device).start()
        row_copy(i, 0).start()

    @pl.when(jnp.logical_not(is_source))
    def _():
        for j in range(n_err // 2):
            err_copy(own(j), to_c, 0).wait_recv()
            err_forward(own(j))

    eye = (lax.broadcasted_iota(jnp.int32, (PANEL, PANEL), 0)
           == lax.broadcasted_iota(jnp.int32, (PANEL, PANEL), 1)).astype(F32)
    block = diag[...]
    trace = jnp.sum(jnp.sum(block * eye, axis=1, keepdims=True), axis=0, keepdims=True)
    shrink = 1.0 / (1.01 * trace)
    scaled[...] = (block + (0.01 / PANEL) * trace * eye) * shrink
    square[...] = eye - scaled[...]
    inverse[...] = eye + square[...]

    def double(_, carry):
        r = square[...]
        r2 = three(r, r)
        square[...] = r2
        x = inverse[...]
        inverse[...] = x + three(x, r2)
        return carry

    steps = -(-SQUARINGS // (n_feat - 1))
    for i in range(n_feat):
        lax.fori_loop(0, steps if i else SQUARINGS - steps * (n_feat - 1), double, 0)
        for k, device in enumerate(peers):
            all_copy(i, n_tok - 2 - k, device).wait_recv()
            row_copy(i, k + 1).start()

    def polish(_, carry):
        x = inverse[...]
        inverse[...] = x + high(eye - high(x, scaled[...]), x)
        return carry

    lax.fori_loop(0, POLISH, polish, 0)
    top, low = split(inverse[...] * shrink)

    def multiply(r, i):
        h_top, h_low = split(hess_ref[r, i])
        w_top, w_low = split(
            jnp.dot(top, h_top, preferred_element_type=F32)
            + jnp.dot(top, h_low, preferred_element_type=F32)
            + jnp.dot(low, h_top, preferred_element_type=F32))
        cols = pl.ds(pl.multiple_of((r * n_feat + i) * width, width), width)
        product_ref[:PANEL, cols] = w_top
        product_ref[PANEL:, cols] = w_low

    for i in range(n_feat):
        multiply(row, i)
    for i in range(n_feat):
        for k in range(n_tok):
            row_copy(i, k).wait_recv()
        multiply(1 - row, i)

    for i in range(n_feat):
        for k, device in enumerate(peers):
            red_copy(i, k, device).wait_send()
            all_copy(i, k, device).wait_send()
        for k in range(n_tok):
            row_copy(i, k).wait_send()

    @pl.when(jnp.logical_not(is_source))
    def _():
        for j in range(n_err // 2):
            err_copy(other(j), to_c, 0).wait_recv()

    def drain(j, carry):
        c = own(j)

        @pl.when(can_z)
        def _():
            send(c, to_z, send_z).wait_send()

        @pl.when(even_y)
        def _():
            send(c, to_y, send_y).wait_send()

        @pl.when(not_twin)
        def _():
            send(c, to_c, send_c).wait_send()

        @pl.when(is_source)
        def _():
            send(other(j), to_c, send_c).wait_send()

        return carry

    lax.fori_loop(0, n_pairs, drain, 0)

    @pl.when(chain_z)
    def _():
        half_copy(core, to_z, 0).wait_send()
        for j in range(n_err // 2):
            err_copy(own(j), to_z, 0).wait_send()

    @pl.when(root_y)
    def _():
        half_copy(core, to_y, 1).wait_send()
        for j in range(n_err // 2):
            err_copy(own(j), to_y_same, 1).wait_send()

    @pl.when(not_twin)
    def _():
        half_copy(core, to_c, 2).wait_send()
        for j in range(n_err // 2):
            err_copy(own(j), to_c, 2).wait_send()

    @pl.when(is_source)
    def _():
        half_copy(1, to_c, 3).wait_send()
        for j in range(n_err // 2):
            err_copy(other(j), to_c, 2).wait_send()
        for k, device in enumerate(peers):
            diag_copy(diag_part, diag_send, diag_recv, tok, k, device).wait_send()


def diag_copy(diag_part, send_sem, recv_sem, tok, k, device):
    n = diag_part.shape[0]
    return pltpu.make_async_remote_copy(
        src_ref=diag_part.at[tok], dst_ref=diag_part.at[tok], send_sem=send_sem.at[k],
        recv_sem=recv_sem.at[n - 2 - k], device_id=device, device_id_type=MESH)


def exchange(quantized, exponents, weights, keep_mask):
    tokens, columns = quantized.shape
    rows = weights.shape[0]
    n_tok = lax.axis_size("tok")
    n_quant = columns // lax.axis_size("row")
    width = 128
    n_feat = n_quant // width
    n_chunks = tokens // CHUNK
    n_err = rows // CHUNK
    strip = PANEL // n_tok
    sizes = (n_chunks, n_chunks // 2, n_err, width, n_feat, n_tok)
    dma = pltpu.SemaphoreType.DMA
    vmem = pl.BlockSpec(memory_space=pltpu.VMEM)
    hbm = pl.BlockSpec(memory_space=pltpu.HBM)
    return pl.pallas_call(
        functools.partial(exchange_kernel, sizes),
        out_shape=(
            jax.ShapeDtypeStruct((2 * PANEL, columns), BF16),
            jax.ShapeDtypeStruct((rows, PANEL), BF16),
        ),
        in_specs=[hbm, hbm, hbm, hbm],
        out_specs=(vmem, vmem),
        scratch_shapes=[
            pltpu.VMEM(exponents.T.shape, jnp.int32),
            pltpu.VMEM((tokens, PANEL), BF16),
            pltpu.VMEM((tokens, PANEL), BF16),
            pltpu.VMEM((tokens, n_quant), BF16),
            pltpu.VMEM((rows, PANEL), BF16),
            pltpu.VMEM((rows, PANEL), jnp.int32),
            pltpu.VMEM((2, n_feat, PANEL, width), F32),
            pltpu.VMEM((n_feat, PANEL, width), F32),
            pltpu.VMEM((n_feat, n_tok, strip, width), F32),
            pltpu.VMEM((n_tok, PANEL, PANEL), F32),
            pltpu.VMEM((PANEL, PANEL), F32),
            pltpu.VMEM((PANEL, PANEL), F32),
            pltpu.VMEM((PANEL, PANEL), F32),
            pltpu.VMEM((PANEL, PANEL), F32),
            dma((3,)), dma((n_chunks,)), dma((n_chunks,)),
            dma((n_chunks,)), dma((n_chunks,)), dma((n_chunks,)),
            dma((n_tok - 1,)), dma((n_tok - 1,)), dma((4,)), dma((2,)),
            dma((3, n_err)), dma((n_err,)),
            dma((n_feat, n_tok - 1)), dma((n_feat, n_tok - 1)),
            dma((n_feat, n_tok - 1)), dma((n_feat, n_tok - 1)),
            dma((n_feat, n_tok)), dma((n_feat, n_tok)),
        ],
        compiler_params=pltpu.CompilerParams(
            collective_id=0, has_side_effects=True, vmem_limit_bytes=32 * 1024 * 1024),
        name="exchange",
    )(*[pltpu.with_memory_space_constraint(x, pltpu.HBM)
        for x in (quantized, exponents.T, weights, keep_mask)])


def update_kernel(feat_ref, product_ref, error_ref, weights_ref, out_ref):
    error = error_ref[...]
    both = jnp.concatenate([error, error], axis=1)
    update = jnp.dot(both, product_ref[...], preferred_element_type=F32)
    out_ref[...] = (weights_ref[...].astype(F32) + update).astype(BF16)

    @pl.when(feat_ref[0] == 0)
    def _():
        out_ref[:, :PANEL] = weights_ref[:, :PANEL] - error


def apply_update(feat, product, error, weights, tile=512):
    rows, columns = weights.shape
    return pl.pallas_call(
        update_kernel,
        grid=(rows // tile,),
        out_shape=jax.ShapeDtypeStruct(weights.shape, BF16),
        in_specs=[
            pl.BlockSpec(memory_space=pltpu.SMEM),
            pl.BlockSpec(memory_space=pltpu.VMEM),
            pl.BlockSpec((tile, PANEL), lambda g: (g, 0)),
            pl.BlockSpec((tile, columns), lambda g: (g, 0)),
        ],
        out_specs=pl.BlockSpec((tile, columns), lambda g: (g, 0)),
        compiler_params=pltpu.CompilerParams(vmem_limit_bytes=24 * 1024 * 1024),
        name="update",
    )(feat, product, error, weights)


def shards(quantized, exponents, weights, keep_mask):
    product, error = exchange(quantized, exponents, weights, keep_mask)
    feat = lax.axis_index("feat").astype(jnp.int32).reshape(1)
    return apply_update(feat, product, error, weights)


def solution(mesh):
    placed = (
        P("tok", "feat"),
        P("tok", "feat"),
        P(("tok", "row"), "feat"),
        P(("tok", "row"), None),
    )
    return jax.shard_map(
        shards, mesh=mesh, in_specs=placed, out_specs=P(("tok", "row"), "feat"), check_vma=False
    )
```

```python
import functools

import jax
import jax.numpy as jnp
from jax import lax
from jax.experimental import pallas as pl
from jax.experimental.pallas import tpu as pltpu
from jax.sharding import PartitionSpec as P

PANEL = 256
QBLOCK = 128
CHUNK = 256
PIECE = 128
LAG = 8
SQUARINGS = 18
POLISH = 2
MESH = pl.DeviceIdType.MESH
F32 = jnp.float32
BF16 = jnp.bfloat16


def high(left, right):
    return jnp.dot(left, right, precision=lax.Precision.HIGHEST, preferred_element_type=F32)


def three(left, right):
    l_top, l_low = split(left)
    r_top, r_low = split(right)
    return (jnp.dot(l_top, r_top, preferred_element_type=F32)
            + jnp.dot(l_top, r_low, preferred_element_type=F32)
            + jnp.dot(l_low, r_top, preferred_element_type=F32))


def split(value):
    top = value.astype(BF16)
    return top, (value - top.astype(F32)).astype(BF16)


def exchange_kernel(
    sizes,
    quant_ref, exps_hbm, weights_ref, keep_ref,
    product_ref, error_out,
    exps_ref, raw, acts, quant, weights, keep, hess_ref, part, summed, diag_part, diag, square, inverse, scaled,
    load_sem, quant_sem, arrive, send_z, send_y, send_c,
    diag_send, diag_recv, half_send, half_recv,
    err_send, err_recv,
    red_send, red_recv, all_send, all_recv, row_send, row_recv,
):
    n_chunks, n_pairs, n_err, width, n_feat, n_tok = sizes
    tok, feat, row = lax.axis_index("tok"), lax.axis_index("feat"), lax.axis_index("row")
    y_lo, z, core = feat // 8, (feat // 2) % 4, feat % 2
    strip = PANEL // n_tok
    n_quant = n_feat * width

    def at(t, y, zz, c, r):
        return (t, (y * 4 + zz) * 2 + c, r)

    z_up, z_down = (z + 1) % 4, (z + 3) % 4
    z_next = core * z_down + (1 - core) * z_up
    hops = core * ((4 - z) % 4) + (1 - core) * z
    cross_row = core * (1 - row) + (1 - core) * row
    to_z = at(tok, y_lo, z_next, core, row)
    to_y = at(tok, 1 - y_lo, z, core, cross_row)
    to_y_same = at(tok, 1 - y_lo, z, core, row)
    to_c = at(tok, y_lo, z, 1 - core, row)
    to_row = (tok, feat, 1 - row)
    peers = [((tok + k) % n_tok, feat, row) for k in range(1, n_tok)]
    greeted = [
        at(tok, y_lo, z_up, core, row), at(tok, y_lo, z_down, core, row),
        at(tok, 1 - y_lo, z, core, 0), at(tok, 1 - y_lo, z, core, 1),
        to_c, to_row,
    ] + peers
    even_y = y_lo == 0
    is_source = feat == 0
    is_twin = feat == 1
    not_twin = feat != 1
    chain_z = hops < 3
    root_y = jnp.logical_and(even_y, z == 0)

    def own(j):
        return 2 * j + core

    def other(j):
        return 2 * j + 1 - core

    def rows_of(c, size=CHUNK):
        return pl.ds(pl.multiple_of(c * size, size), size)

    def load(c):
        return pltpu.make_async_copy(
            quant_ref.at[rows_of(c), pl.ds(0, PANEL)], raw.at[rows_of(c)], arrive.at[c])

    def error_load():
        return (pltpu.make_async_copy(weights_ref.at[:, pl.ds(0, PANEL)], weights, load_sem.at[0]),
                pltpu.make_async_copy(keep_ref, keep, load_sem.at[1]))

    def scales_of(c):
        exps = exps_ref[:, rows_of(c)].astype(F32)
        return jnp.exp2(exps).T

    def spread(column):
        return jnp.broadcast_to(column, (CHUNK, QBLOCK)).astype(BF16)

    def hub(j):
        return 2 * own(j) + y_lo

    def leaf(j):
        return 2 * own(j) + 1 - y_lo

    def send(p, target, sem):
        piece = acts.at[rows_of(p, PIECE)]
        return pltpu.make_async_remote_copy(
            src_ref=piece, dst_ref=piece, send_sem=sem.at[p], recv_sem=arrive.at[p],
            device_id=target, device_id_type=MESH)

    def quant_load(c):
        cols = pl.ds(pl.multiple_of(row * n_quant, 128), n_quant)
        return pltpu.make_async_copy(
            quant_ref.at[rows_of(c), cols], quant.at[rows_of(c)], quant_sem.at[c])

    exps_copy = pltpu.make_async_copy(exps_hbm, exps_ref, load_sem.at[2])
    exps_copy.start()

    @pl.when(is_source)
    def _():
        for c in range(n_chunks):
            load(c).start()
        for copy in error_load():
            copy.start()

    for c in range(n_chunks):
        quant_load(c).start()

    barrier = pltpu.get_barrier_semaphore()
    for device in greeted:
        pl.semaphore_signal(barrier, inc=1, device_id=device, device_id_type=MESH)
    pl.semaphore_wait(barrier, len(greeted))
    exps_copy.wait()

    def hub_forward(j):
        @pl.when(chain_z)
        def _():
            send(hub(j), to_z, send_z).start()

        @pl.when(z != 0)
        def _():
            send(hub(j), to_y, send_y).start()

        @pl.when(not_twin)
        def _():
            send(hub(j), to_c, send_c).start()

    def leaf_forward(j):
        @pl.when(root_y)
        def _():
            send(leaf(j), to_y, send_y).start()

        @pl.when(not_twin)
        def _():
            send(leaf(j), to_c, send_c).start()

    def late_forward(j, carry):
        send(hub(j), to_y, send_y).start()
        return carry

    def half_copy(h, target, slot):
        return pltpu.make_async_remote_copy(
            src_ref=diag.at[rows_of(h, PANEL // 2)], dst_ref=diag.at[rows_of(h, PANEL // 2)],
            send_sem=half_send.at[slot], recv_sem=half_recv.at[h],
            device_id=target, device_id_type=MESH)

    def err_copy(c, target, slot):
        return pltpu.make_async_remote_copy(
            src_ref=error_out.at[rows_of(c)], dst_ref=error_out.at[rows_of(c)],
            send_sem=err_send.at[slot, c], recv_sem=err_recv.at[c],
            device_id=target, device_id_type=MESH)

    def half_forward():
        @pl.when(chain_z)
        def _():
            half_copy(core, to_z, 0).start()

        @pl.when(root_y)
        def _():
            half_copy(core, to_y, 1).start()

        @pl.when(not_twin)
        def _():
            half_copy(core, to_c, 2).start()

    def err_forward(c):
        @pl.when(chain_z)
        def _():
            err_copy(c, to_z, 0).start()

        @pl.when(root_y)
        def _():
            err_copy(c, to_y_same, 1).start()

        @pl.when(not_twin)
        def _():
            err_copy(c, to_c, 2).start()

    @pl.when(is_source)
    def _():
        def scale(c):
            load(c).wait()
            scales = scales_of(c)
            for b in range(PANEL // QBLOCK):
                cols = slice(b * QBLOCK, (b + 1) * QBLOCK)
                acts[rows_of(c), cols] = raw[rows_of(c), cols] * spread(scales[:, b:b + 1])

        def pass_on(j):
            hub_forward(j)
            leaf_forward(j)
            for half in range(2):
                send(2 * other(j) + half, to_c, send_c).start()

        def body(j, carry):
            scale(own(j))
            scale(other(j))
            pass_on(j - 1)
            return carry

        scale(0)
        scale(1)
        lax.fori_loop(1, n_pairs, body, 0)
        pass_on(n_pairs - 1)
        lax.fori_loop(0, n_pairs, late_forward, 0)

        def gram(c, carry):
            block = acts[rows_of(c), :]
            term = lax.dot_general(block, block, (((0,), (0,)), ((), ())), preferred_element_type=F32)

            @pl.when(c == 0)
            def _():
                diag_part[tok] = term

            @pl.when(c > 0)
            def _():
                diag_part[tok] += term

            return carry

        lax.fori_loop(0, n_chunks, gram, 0)
        for k, device in enumerate(peers):
            diag_copy(diag_part, diag_send, diag_recv, tok, k, device).start()

    def prescale(c):
        quant_load(c).wait()
        scales = scales_of(c)
        n_blocks = n_quant // QBLOCK
        for b in range(n_blocks):
            cols = slice(b * QBLOCK, (b + 1) * QBLOCK)
            column = jnp.where(row == 0, scales[:, b:b + 1], scales[:, n_blocks + b:n_blocks + b + 1])
            quant[rows_of(c), cols] = quant[rows_of(c), cols] * spread(column)

    def accumulate(c):
        term = lax.dot_general(
            acts[rows_of(c), :], quant[rows_of(c), :], (((0,), (0,)), ((), ())),
            preferred_element_type=F32)
        for i in range(n_feat):
            part[i] += term[:, i * width:(i + 1) * width]

    def own_gram(j):
        @pl.when(feat > 1)
        def _():
            send(leaf(j), to_c, send_c).wait_recv()
            leaf_forward(j)

        accumulate(own(j))

    part[...] = jnp.zeros_like(part)

    def hub_step(j, carry):
        @pl.when(jnp.logical_not(is_source))
        def _():
            send(hub(j), to_c, send_c).wait_recv()
            hub_forward(j)

        @pl.when(is_twin)
        def _():
            send(leaf(j), to_c, send_c).wait_recv()
            leaf_forward(j)

        @pl.when(jnp.logical_and(j >= LAG, feat > 1))
        def _():
            own_gram(j - LAG)

        return carry

    def prescale_step(c, carry):
        prescale(c)
        return carry

    lax.fori_loop(0, jnp.where(feat > 1, n_chunks, 0), prescale_step, 0)
    lax.fori_loop(0, n_pairs, hub_step, 0)

    @pl.when(is_twin)
    def _():
        lax.fori_loop(0, n_pairs, late_forward, 0)

    lax.fori_loop(jnp.where(feat > 1, n_chunks, 0), n_chunks, prescale_step, 0)

    def own_step(j, carry):
        own_gram(j)
        return carry

    @pl.when(is_source)
    def _():
        for k, device in enumerate(peers):
            diag_copy(diag_part, diag_send, diag_recv, tok, k, device).wait_recv()
        total = diag_part[0]
        for t in range(1, n_tok):
            total = total + diag_part[t]
        diag[...] = total
        for copy in error_load():
            copy.wait()
        error_out[...] = jnp.where(keep[...] == 0, weights[...].astype(F32), 0.0).astype(BF16)
        half_forward()
        half_copy(1, to_c, 3).start()

    lax.fori_loop(jnp.where(feat > 1, n_pairs - LAG, 0), n_pairs, own_step, 0)

    def other_step(j, carry):
        @pl.when(jnp.logical_not(is_source))
        def _():
            for half in range(2):
                send(2 * other(j) + half, to_c, send_c).wait_recv()

        accumulate(other(j))
        return carry

    lax.fori_loop(0, n_pairs, other_step, 0)

    @pl.when(is_source)
    def _():
        for j in range(n_err // 2):
            err_forward(own(j))
            err_copy(other(j), to_c, 2).start()

    def red_copy(i, k, device):
        dest = device[0]
        return pltpu.make_async_remote_copy(
            src_ref=part.at[i, rows_of(dest, strip)], dst_ref=summed.at[i, tok],
            send_sem=red_send.at[i, k], recv_sem=red_recv.at[i, n_tok - 2 - k],
            device_id=device, device_id_type=MESH)

    for i in range(n_feat):
        for k, device in enumerate(peers):
            red_copy(i, k, device).start()

    @pl.when(jnp.logical_not(is_source))
    def _():
        half_copy(core, to_c, 0).wait_recv()
        half_forward()
        half_copy(1 - core, to_c, 0).wait_recv()

    def all_copy(i, k, device):
        piece = hess_ref.at[row, i, rows_of(tok, strip)]
        return pltpu.make_async_remote_copy(
            src_ref=piece, dst_ref=piece, send_sem=all_send.at[i, k],
            recv_sem=all_recv.at[i, n_tok - 2 - k], device_id=device, device_id_type=MESH)

    def row_copy(i, k):
        owner = (tok + k) % n_tok
        piece = hess_ref.at[row, i, rows_of(owner, strip)]
        return pltpu.make_async_remote_copy(
            src_ref=piece, dst_ref=piece, send_sem=row_send.at[i, k],
            recv_sem=row_recv.at[i, k], device_id=to_row, device_id_type=MESH)

    for i in range(n_feat):
        for k, device in enumerate(peers):
            red_copy(i, k, device).wait_recv()
        mine = part[i, rows_of(tok, strip), :]
        for k in range(1, n_tok):
            mine = mine + summed[i, (tok + k) % n_tok]
        hess_ref[row, i, rows_of(tok, strip), :] = mine
        for k, device in enumerate(peers):
            all_copy(i, k, device).start()
        row_copy(i, 0).start()

    def err_pass(ready):
        @pl.when(jnp.logical_and(ready, jnp.logical_not(is_source)))
        def _():
            for j in range(n_err // 2):
                err_copy(own(j), to_c, 0).wait_recv()
                err_forward(own(j))

    err_pass(hops <= 1)

    eye = (lax.broadcasted_iota(jnp.int32, (PANEL, PANEL), 0)
           == lax.broadcasted_iota(jnp.int32, (PANEL, PANEL), 1)).astype(F32)
    block = diag[...]
    trace = jnp.sum(jnp.sum(block * eye, axis=1, keepdims=True), axis=0, keepdims=True)
    shrink = 1.0 / (1.01 * trace)
    scaled[...] = (block + (0.01 / PANEL) * trace * eye) * shrink
    square[...] = eye - scaled[...]
    inverse[...] = eye + square[...]

    def double(_, carry):
        r = square[...]
        r2 = three(r, r)
        square[...] = r2
        x = inverse[...]
        inverse[...] = x + three(x, r2)
        return carry

    steps = -(-SQUARINGS // (n_feat - 1))
    for i in range(n_feat):
        lax.fori_loop(0, steps if i else SQUARINGS - steps * (n_feat - 1), double, 0)
        if i == 2:
            err_pass(hops == 2)
        if i == 5:
            err_pass(hops == 3)
        for k, device in enumerate(peers):
            all_copy(i, n_tok - 2 - k, device).wait_recv()
            row_copy(i, k + 1).start()

    def polish(_, carry):
        x = inverse[...]
        inverse[...] = x + high(eye - high(x, scaled[...]), x)
        return carry

    lax.fori_loop(0, POLISH, polish, 0)
    top, low = split(inverse[...] * shrink)

    def multiply(r, i):
        h_top, h_low = split(hess_ref[r, i])
        w_top, w_low = split(
            jnp.dot(top, h_top, preferred_element_type=F32)
            + jnp.dot(top, h_low, preferred_element_type=F32)
            + jnp.dot(low, h_top, preferred_element_type=F32))
        cols = pl.ds(pl.multiple_of((r * n_feat + i) * width, width), width)
        product_ref[:PANEL, cols] = w_top
        product_ref[PANEL:, cols] = w_low

    for i in range(n_feat):
        multiply(row, i)
    for i in range(n_feat):
        for k in range(n_tok):
            row_copy(i, k).wait_recv()
        multiply(1 - row, i)

    for i in range(n_feat):
        for k, device in enumerate(peers):
            red_copy(i, k, device).wait_send()
            all_copy(i, k, device).wait_send()
        for k in range(n_tok):
            row_copy(i, k).wait_send()

    @pl.when(jnp.logical_not(is_source))
    def _():
        for j in range(n_err // 2):
            err_copy(other(j), to_c, 0).wait_recv()

    def drain(j, carry):
        @pl.when(chain_z)
        def _():
            send(hub(j), to_z, send_z).wait_send()

        @pl.when(jnp.logical_or(even_y, z != 0))
        def _():
            send(hub(j), to_y, send_y).wait_send()

        @pl.when(root_y)
        def _():
            send(leaf(j), to_y, send_y).wait_send()

        @pl.when(not_twin)
        def _():
            send(hub(j), to_c, send_c).wait_send()
            send(leaf(j), to_c, send_c).wait_send()

        @pl.when(is_source)
        def _():
            for half in range(2):
                send(2 * other(j) + half, to_c, send_c).wait_send()

        return carry

    lax.fori_loop(0, n_pairs, drain, 0)

    @pl.when(chain_z)
    def _():
        half_copy(core, to_z, 0).wait_send()
        for j in range(n_err // 2):
            err_copy(own(j), to_z, 0).wait_send()

    @pl.when(root_y)
    def _():
        half_copy(core, to_y, 1).wait_send()
        for j in range(n_err // 2):
            err_copy(own(j), to_y_same, 1).wait_send()

    @pl.when(not_twin)
    def _():
        half_copy(core, to_c, 2).wait_send()
        for j in range(n_err // 2):
            err_copy(own(j), to_c, 2).wait_send()

    @pl.when(is_source)
    def _():
        half_copy(1, to_c, 3).wait_send()
        for j in range(n_err // 2):
            err_copy(other(j), to_c, 2).wait_send()
        for k, device in enumerate(peers):
            diag_copy(diag_part, diag_send, diag_recv, tok, k, device).wait_send()


def diag_copy(diag_part, send_sem, recv_sem, tok, k, device):
    n = diag_part.shape[0]
    return pltpu.make_async_remote_copy(
        src_ref=diag_part.at[tok], dst_ref=diag_part.at[tok], send_sem=send_sem.at[k],
        recv_sem=recv_sem.at[n - 2 - k], device_id=device, device_id_type=MESH)


def exchange(quantized, exponents, weights, keep_mask):
    tokens, columns = quantized.shape
    rows = weights.shape[0]
    n_tok = lax.axis_size("tok")
    n_quant = columns // lax.axis_size("row")
    width = 128
    n_feat = n_quant // width
    n_chunks = tokens // CHUNK
    n_pieces = tokens // PIECE
    n_err = rows // CHUNK
    strip = PANEL // n_tok
    sizes = (n_chunks, n_chunks // 2, n_err, width, n_feat, n_tok)
    dma = pltpu.SemaphoreType.DMA
    vmem = pl.BlockSpec(memory_space=pltpu.VMEM)
    hbm = pl.BlockSpec(memory_space=pltpu.HBM)
    return pl.pallas_call(
        functools.partial(exchange_kernel, sizes),
        out_shape=(
            jax.ShapeDtypeStruct((2 * PANEL, columns), BF16),
            jax.ShapeDtypeStruct((rows, PANEL), BF16),
        ),
        in_specs=[hbm, hbm, hbm, hbm],
        out_specs=(vmem, vmem),
        scratch_shapes=[
            pltpu.VMEM(exponents.T.shape, jnp.int32),
            pltpu.VMEM((tokens, PANEL), BF16),
            pltpu.VMEM((tokens, PANEL), BF16),
            pltpu.VMEM((tokens, n_quant), BF16),
            pltpu.VMEM((rows, PANEL), BF16),
            pltpu.VMEM((rows, PANEL), jnp.int32),
            pltpu.VMEM((2, n_feat, PANEL, width), F32),
            pltpu.VMEM((n_feat, PANEL, width), F32),
            pltpu.VMEM((n_feat, n_tok, strip, width), F32),
            pltpu.VMEM((n_tok, PANEL, PANEL), F32),
            pltpu.VMEM((PANEL, PANEL), F32),
            pltpu.VMEM((PANEL, PANEL), F32),
            pltpu.VMEM((PANEL, PANEL), F32),
            pltpu.VMEM((PANEL, PANEL), F32),
            dma((3,)), dma((n_chunks,)), dma((n_pieces,)),
            dma((n_pieces,)), dma((n_pieces,)), dma((n_pieces,)),
            dma((n_tok - 1,)), dma((n_tok - 1,)), dma((4,)), dma((2,)),
            dma((3, n_err)), dma((n_err,)),
            dma((n_feat, n_tok - 1)), dma((n_feat, n_tok - 1)),
            dma((n_feat, n_tok - 1)), dma((n_feat, n_tok - 1)),
            dma((n_feat, n_tok)), dma((n_feat, n_tok)),
        ],
        compiler_params=pltpu.CompilerParams(
            collective_id=0, has_side_effects=True, vmem_limit_bytes=32 * 1024 * 1024),
        name="exchange",
    )(*[pltpu.with_memory_space_constraint(x, pltpu.HBM)
        for x in (quantized, exponents.T, weights, keep_mask)])


def update_kernel(feat_ref, product_ref, error_ref, weights_ref, out_ref):
    error = error_ref[...]
    both = jnp.concatenate([error, error], axis=1)
    update = jnp.dot(both, product_ref[...], preferred_element_type=F32)
    out_ref[...] = (weights_ref[...].astype(F32) + update).astype(BF16)

    @pl.when(feat_ref[0] == 0)
    def _():
        out_ref[:, :PANEL] = weights_ref[:, :PANEL] - error


def apply_update(feat, product, error, weights, tile=512):
    rows, columns = weights.shape
    return pl.pallas_call(
        update_kernel,
        grid=(rows // tile,),
        out_shape=jax.ShapeDtypeStruct(weights.shape, BF16),
        in_specs=[
            pl.BlockSpec(memory_space=pltpu.SMEM),
            pl.BlockSpec(memory_space=pltpu.VMEM),
            pl.BlockSpec((tile, PANEL), lambda g: (g, 0)),
            pl.BlockSpec((tile, columns), lambda g: (g, 0)),
        ],
        out_specs=pl.BlockSpec((tile, columns), lambda g: (g, 0)),
        compiler_params=pltpu.CompilerParams(vmem_limit_bytes=24 * 1024 * 1024),
        name="update",
    )(feat, product, error, weights)


def shards(quantized, exponents, weights, keep_mask):
    product, error = exchange(quantized, exponents, weights, keep_mask)
    feat = lax.axis_index("feat").astype(jnp.int32).reshape(1)
    return apply_update(feat, product, error, weights)


def solution(mesh):
    placed = (
        P("tok", "feat"),
        P("tok", "feat"),
        P(("tok", "row"), "feat"),
        P(("tok", "row"), None),
    )
    return jax.shard_map(
        shards, mesh=mesh, in_specs=placed, out_specs=P(("tok", "row"), "feat"), check_vma=False
    )
```

```python
import functools

import jax
import jax.numpy as jnp
from jax import lax
from jax.experimental import pallas as pl
from jax.experimental.pallas import tpu as pltpu
from jax.sharding import PartitionSpec as P

PANEL = 256
QBLOCK = 128
CHUNK = 256
PIECE = 128
LAG = 5
SQUARINGS = 18
POLISH = 2
MESH = pl.DeviceIdType.MESH
F32 = jnp.float32
BF16 = jnp.bfloat16


def high(left, right):
    return jnp.dot(left, right, precision=lax.Precision.HIGHEST, preferred_element_type=F32)


def three(left, right):
    l_top, l_low = split(left)
    r_top, r_low = split(right)
    return (jnp.dot(l_top, r_top, preferred_element_type=F32)
            + jnp.dot(l_top, r_low, preferred_element_type=F32)
            + jnp.dot(l_low, r_top, preferred_element_type=F32))


def split(value):
    top = value.astype(BF16)
    return top, (value - top.astype(F32)).astype(BF16)


def exchange_kernel(
    sizes,
    quant_ref, exps_hbm, weights_ref, keep_ref,
    product_ref, error_out,
    exps_ref, raw, acts, quant, weights, keep, hess_ref, part, summed, diag_part, diag, square, inverse, scaled,
    load_sem, quant_sem, arrive, send_z, send_y, send_c,
    diag_send, diag_recv, half_send, half_recv,
    err_send, err_recv,
    red_send, red_recv, all_send, all_recv, row_send, row_recv,
):
    n_chunks, n_pairs, n_err, width, n_feat, n_tok = sizes
    tok, feat, row = lax.axis_index("tok"), lax.axis_index("feat"), lax.axis_index("row")
    y_lo, z, core = feat // 8, (feat // 2) % 4, feat % 2
    strip = PANEL // n_tok
    n_quant = n_feat * width

    def at(t, y, zz, c, r):
        return (t, (y * 4 + zz) * 2 + c, r)

    z_up, z_down = (z + 1) % 4, (z + 3) % 4
    z_next = core * z_down + (1 - core) * z_up
    hops = core * ((4 - z) % 4) + (1 - core) * z
    cross_row = core * (1 - row) + (1 - core) * row
    to_z = at(tok, y_lo, z_next, core, row)
    to_y = at(tok, 1 - y_lo, z, core, cross_row)
    to_y_same = at(tok, 1 - y_lo, z, core, row)
    to_c = at(tok, y_lo, z, 1 - core, row)
    to_row = (tok, feat, 1 - row)
    peers = [((tok + k) % n_tok, feat, row) for k in range(1, n_tok)]
    greeted = [
        at(tok, y_lo, z_up, core, row), at(tok, y_lo, z_down, core, row),
        at(tok, 1 - y_lo, z, core, 0), at(tok, 1 - y_lo, z, core, 1),
        to_c, to_row,
    ] + peers
    even_y = y_lo == 0
    is_source = feat == 0
    is_twin = feat == 1
    not_twin = feat != 1
    chain_z = hops < 3
    root_y = jnp.logical_and(even_y, z == 0)

    def own(j):
        return 2 * j + core

    def other(j):
        return 2 * j + 1 - core

    def rows_of(c, size=CHUNK):
        return pl.ds(pl.multiple_of(c * size, size), size)

    def load(c):
        return pltpu.make_async_copy(
            quant_ref.at[rows_of(c), pl.ds(0, PANEL)], raw.at[rows_of(c)], arrive.at[c])

    def error_load():
        return (pltpu.make_async_copy(weights_ref.at[:, pl.ds(0, PANEL)], weights, load_sem.at[0]),
                pltpu.make_async_copy(keep_ref, keep, load_sem.at[1]))

    def scales_of(c):
        exps = exps_ref[:, rows_of(c)].astype(F32)
        return jnp.exp2(exps).T

    def spread(column):
        return jnp.broadcast_to(column, (CHUNK, QBLOCK)).astype(BF16)

    def hub(j):
        return 2 * own(j) + y_lo

    def leaf(j):
        return 2 * own(j) + 1 - y_lo

    def send(p, target, sem):
        piece = acts.at[rows_of(p, PIECE)]
        return pltpu.make_async_remote_copy(
            src_ref=piece, dst_ref=piece, send_sem=sem.at[p], recv_sem=arrive.at[p],
            device_id=target, device_id_type=MESH)

    def quant_load(c):
        cols = pl.ds(pl.multiple_of(row * n_quant, 128), n_quant)
        return pltpu.make_async_copy(
            quant_ref.at[rows_of(c), cols], quant.at[rows_of(c)], quant_sem.at[c])

    exps_copy = pltpu.make_async_copy(exps_hbm, exps_ref, load_sem.at[2])
    exps_copy.start()

    @pl.when(is_source)
    def _():
        for c in range(n_chunks):
            load(c).start()
        for copy in error_load():
            copy.start()

    for c in range(n_chunks):
        quant_load(c).start()

    barrier = pltpu.get_barrier_semaphore()
    for device in greeted:
        pl.semaphore_signal(barrier, inc=1, device_id=device, device_id_type=MESH)
    pl.semaphore_wait(barrier, len(greeted))
    exps_copy.wait()

    def hub_forward(j):
        @pl.when(chain_z)
        def _():
            send(hub(j), to_z, send_z).start()

        @pl.when(z != 0)
        def _():
            send(hub(j), to_y, send_y).start()

        @pl.when(not_twin)
        def _():
            send(hub(j), to_c, send_c).start()

    def leaf_forward(j):
        @pl.when(root_y)
        def _():
            send(leaf(j), to_y, send_y).start()

        @pl.when(not_twin)
        def _():
            send(leaf(j), to_c, send_c).start()

    def late_forward(j, carry):
        send(hub(j), to_y, send_y).start()
        return carry

    def half_copy(h, target, slot):
        return pltpu.make_async_remote_copy(
            src_ref=diag.at[rows_of(h, PANEL // 2)], dst_ref=diag.at[rows_of(h, PANEL // 2)],
            send_sem=half_send.at[slot], recv_sem=half_recv.at[h],
            device_id=target, device_id_type=MESH)

    def err_copy(c, target, slot):
        return pltpu.make_async_remote_copy(
            src_ref=error_out.at[rows_of(c)], dst_ref=error_out.at[rows_of(c)],
            send_sem=err_send.at[slot, c], recv_sem=err_recv.at[c],
            device_id=target, device_id_type=MESH)

    def half_forward():
        @pl.when(chain_z)
        def _():
            half_copy(core, to_z, 0).start()

        @pl.when(root_y)
        def _():
            half_copy(core, to_y, 1).start()

        @pl.when(not_twin)
        def _():
            half_copy(core, to_c, 2).start()

    def err_forward(c):
        @pl.when(chain_z)
        def _():
            err_copy(c, to_z, 0).start()

        @pl.when(root_y)
        def _():
            err_copy(c, to_y_same, 1).start()

        @pl.when(not_twin)
        def _():
            err_copy(c, to_c, 2).start()

    @pl.when(is_source)
    def _():
        def scale(c):
            load(c).wait()
            scales = scales_of(c)
            for b in range(PANEL // QBLOCK):
                cols = slice(b * QBLOCK, (b + 1) * QBLOCK)
                acts[rows_of(c), cols] = raw[rows_of(c), cols] * spread(scales[:, b:b + 1])

        def pass_on(j):
            hub_forward(j)
            leaf_forward(j)
            for half in range(2):
                send(2 * other(j) + half, to_c, send_c).start()

        def body(j, carry):
            scale(own(j))
            scale(other(j))
            pass_on(j - 1)
            return carry

        scale(0)
        scale(1)
        lax.fori_loop(1, n_pairs, body, 0)
        pass_on(n_pairs - 1)
        lax.fori_loop(0, n_pairs, late_forward, 0)

        def gram(c, carry):
            block = acts[rows_of(c), :]
            term = lax.dot_general(block, block, (((0,), (0,)), ((), ())), preferred_element_type=F32)

            @pl.when(c == 0)
            def _():
                diag_part[tok] = term

            @pl.when(c > 0)
            def _():
                diag_part[tok] += term

            return carry

        lax.fori_loop(0, n_chunks, gram, 0)
        for k, device in enumerate(peers):
            diag_copy(diag_part, diag_send, diag_recv, tok, k, device).start()

    def prescale(c):
        quant_load(c).wait()
        scales = scales_of(c)
        n_blocks = n_quant // QBLOCK
        for b in range(n_blocks):
            cols = slice(b * QBLOCK, (b + 1) * QBLOCK)
            column = jnp.where(row == 0, scales[:, b:b + 1], scales[:, n_blocks + b:n_blocks + b + 1])
            quant[rows_of(c), cols] = quant[rows_of(c), cols] * spread(column)

    def accumulate(c):
        term = lax.dot_general(
            acts[rows_of(c), :], quant[rows_of(c), :], (((0,), (0,)), ((), ())),
            preferred_element_type=F32)
        for i in range(n_feat):
            part[i] += term[:, i * width:(i + 1) * width]

    def own_gram(j):
        @pl.when(feat > 1)
        def _():
            send(leaf(j), to_c, send_c).wait_recv()
            leaf_forward(j)

        accumulate(own(j))

    part[...] = jnp.zeros_like(part)

    def hub_step(j, carry):
        @pl.when(jnp.logical_not(is_source))
        def _():
            send(hub(j), to_c, send_c).wait_recv()
            hub_forward(j)

        @pl.when(is_twin)
        def _():
            send(leaf(j), to_c, send_c).wait_recv()
            leaf_forward(j)

        @pl.when(jnp.logical_and(j >= LAG, feat > 1))
        def _():
            own_gram(j - LAG)

        return carry

    def prescale_step(c, carry):
        prescale(c)
        return carry

    lax.fori_loop(0, jnp.where(feat > 1, n_chunks, 0), prescale_step, 0)
    lax.fori_loop(0, n_pairs, hub_step, 0)

    @pl.when(is_twin)
    def _():
        lax.fori_loop(0, n_pairs, late_forward, 0)

    lax.fori_loop(jnp.where(feat > 1, n_chunks, 0), n_chunks, prescale_step, 0)

    def own_step(j, carry):
        own_gram(j)
        return carry

    @pl.when(is_source)
    def _():
        for k, device in enumerate(peers):
            diag_copy(diag_part, diag_send, diag_recv, tok, k, device).wait_recv()
        total = diag_part[0]
        for t in range(1, n_tok):
            total = total + diag_part[t]
        diag[...] = total
        for copy in error_load():
            copy.wait()
        error_out[...] = jnp.where(keep[...] == 0, weights[...].astype(F32), 0.0).astype(BF16)
        half_forward()
        half_copy(1, to_c, 3).start()

    lax.fori_loop(jnp.where(feat > 1, n_pairs - LAG, 0), n_pairs, own_step, 0)

    def other_step(j, carry):
        @pl.when(jnp.logical_not(is_source))
        def _():
            for half in range(2):
                send(2 * other(j) + half, to_c, send_c).wait_recv()

        accumulate(other(j))
        return carry

    lax.fori_loop(0, n_pairs, other_step, 0)

    @pl.when(is_source)
    def _():
        for j in range(n_err // 2):
            err_forward(own(j))
            err_copy(other(j), to_c, 2).start()

    def red_copy(i, k, device):
        dest = device[0]
        return pltpu.make_async_remote_copy(
            src_ref=part.at[i, rows_of(dest, strip)], dst_ref=summed.at[i, tok],
            send_sem=red_send.at[i, k], recv_sem=red_recv.at[i, n_tok - 2 - k],
            device_id=device, device_id_type=MESH)

    for i in range(n_feat):
        for k, device in enumerate(peers):
            red_copy(i, k, device).start()

    @pl.when(jnp.logical_not(is_source))
    def _():
        half_copy(core, to_c, 0).wait_recv()
        half_forward()
        half_copy(1 - core, to_c, 0).wait_recv()

    def all_copy(i, k, device):
        piece = hess_ref.at[row, i, rows_of(tok, strip)]
        return pltpu.make_async_remote_copy(
            src_ref=piece, dst_ref=piece, send_sem=all_send.at[i, k],
            recv_sem=all_recv.at[i, n_tok - 2 - k], device_id=device, device_id_type=MESH)

    def row_copy(i, k):
        owner = (tok + k) % n_tok
        piece = hess_ref.at[row, i, rows_of(owner, strip)]
        return pltpu.make_async_remote_copy(
            src_ref=piece, dst_ref=piece, send_sem=row_send.at[i, k],
            recv_sem=row_recv.at[i, k], device_id=to_row, device_id_type=MESH)

    for i in range(n_feat):
        for k, device in enumerate(peers):
            red_copy(i, k, device).wait_recv()
        mine = part[i, rows_of(tok, strip), :]
        for k in range(1, n_tok):
            mine = mine + summed[i, (tok + k) % n_tok]
        hess_ref[row, i, rows_of(tok, strip), :] = mine
        for k, device in enumerate(peers):
            all_copy(i, k, device).start()
        row_copy(i, 0).start()

    def err_pass(ready):
        @pl.when(jnp.logical_and(ready, jnp.logical_not(is_source)))
        def _():
            for j in range(n_err // 2):
                err_copy(own(j), to_c, 0).wait_recv()
                err_forward(own(j))

    err_pass(hops <= 1)

    eye = (lax.broadcasted_iota(jnp.int32, (PANEL, PANEL), 0)
           == lax.broadcasted_iota(jnp.int32, (PANEL, PANEL), 1)).astype(F32)
    block = diag[...]
    trace = jnp.sum(jnp.sum(block * eye, axis=1, keepdims=True), axis=0, keepdims=True)
    shrink = 1.0 / (1.01 * trace)
    scaled[...] = (block + (0.01 / PANEL) * trace * eye) * shrink
    square[...] = eye - scaled[...]
    inverse[...] = eye + square[...]

    def double(_, carry):
        r = square[...]
        r2 = three(r, r)
        square[...] = r2
        x = inverse[...]
        inverse[...] = x + three(x, r2)
        return carry

    steps = -(-SQUARINGS // (n_feat - 1))
    for i in range(n_feat):
        lax.fori_loop(0, steps if i else SQUARINGS - steps * (n_feat - 1), double, 0)
        if i == 3:
            err_pass(hops == 2)
        if i == 6:
            err_pass(hops == 3)
        for k, device in enumerate(peers):
            all_copy(i, n_tok - 2 - k, device).wait_recv()
            row_copy(i, k + 1).start()

    def polish(_, carry):
        x = inverse[...]
        inverse[...] = x + high(eye - high(x, scaled[...]), x)
        return carry

    lax.fori_loop(0, POLISH, polish, 0)
    top, low = split(inverse[...] * shrink)

    def multiply(r, i):
        h_top, h_low = split(hess_ref[r, i])
        w_top, w_low = split(
            jnp.dot(top, h_top, preferred_element_type=F32)
            + jnp.dot(top, h_low, preferred_element_type=F32)
            + jnp.dot(low, h_top, preferred_element_type=F32))
        cols = pl.ds(pl.multiple_of((r * n_feat + i) * width, width), width)
        product_ref[:PANEL, cols] = w_top
        product_ref[PANEL:, cols] = w_low

    for i in range(n_feat):
        multiply(row, i)
    for i in range(n_feat):
        for k in range(n_tok):
            row_copy(i, k).wait_recv()
        multiply(1 - row, i)

    for i in range(n_feat):
        for k, device in enumerate(peers):
            red_copy(i, k, device).wait_send()
            all_copy(i, k, device).wait_send()
        for k in range(n_tok):
            row_copy(i, k).wait_send()

    @pl.when(jnp.logical_not(is_source))
    def _():
        for j in range(n_err // 2):
            err_copy(other(j), to_c, 0).wait_recv()

    def drain(j, carry):
        @pl.when(chain_z)
        def _():
            send(hub(j), to_z, send_z).wait_send()

        @pl.when(jnp.logical_or(even_y, z != 0))
        def _():
            send(hub(j), to_y, send_y).wait_send()

        @pl.when(root_y)
        def _():
            send(leaf(j), to_y, send_y).wait_send()

        @pl.when(not_twin)
        def _():
            send(hub(j), to_c, send_c).wait_send()
            send(leaf(j), to_c, send_c).wait_send()

        @pl.when(is_source)
        def _():
            for half in range(2):
                send(2 * other(j) + half, to_c, send_c).wait_send()

        return carry

    lax.fori_loop(0, n_pairs, drain, 0)

    @pl.when(chain_z)
    def _():
        half_copy(core, to_z, 0).wait_send()
        for j in range(n_err // 2):
            err_copy(own(j), to_z, 0).wait_send()

    @pl.when(root_y)
    def _():
        half_copy(core, to_y, 1).wait_send()
        for j in range(n_err // 2):
            err_copy(own(j), to_y_same, 1).wait_send()

    @pl.when(not_twin)
    def _():
        half_copy(core, to_c, 2).wait_send()
        for j in range(n_err // 2):
            err_copy(own(j), to_c, 2).wait_send()

    @pl.when(is_source)
    def _():
        half_copy(1, to_c, 3).wait_send()
        for j in range(n_err // 2):
            err_copy(other(j), to_c, 2).wait_send()
        for k, device in enumerate(peers):
            diag_copy(diag_part, diag_send, diag_recv, tok, k, device).wait_send()


def diag_copy(diag_part, send_sem, recv_sem, tok, k, device):
    n = diag_part.shape[0]
    return pltpu.make_async_remote_copy(
        src_ref=diag_part.at[tok], dst_ref=diag_part.at[tok], send_sem=send_sem.at[k],
        recv_sem=recv_sem.at[n - 2 - k], device_id=device, device_id_type=MESH)


def exchange(quantized, exponents, weights, keep_mask):
    tokens, columns = quantized.shape
    rows = weights.shape[0]
    n_tok = lax.axis_size("tok")
    n_quant = columns // lax.axis_size("row")
    width = 128
    n_feat = n_quant // width
    n_chunks = tokens // CHUNK
    n_pieces = tokens // PIECE
    n_err = rows // CHUNK
    strip = PANEL // n_tok
    sizes = (n_chunks, n_chunks // 2, n_err, width, n_feat, n_tok)
    dma = pltpu.SemaphoreType.DMA
    vmem = pl.BlockSpec(memory_space=pltpu.VMEM)
    hbm = pl.BlockSpec(memory_space=pltpu.HBM)
    return pl.pallas_call(
        functools.partial(exchange_kernel, sizes),
        out_shape=(
            jax.ShapeDtypeStruct((2 * PANEL, columns), BF16),
            jax.ShapeDtypeStruct((rows, PANEL), BF16),
        ),
        in_specs=[hbm, hbm, hbm, hbm],
        out_specs=(vmem, vmem),
        scratch_shapes=[
            pltpu.VMEM(exponents.T.shape, jnp.int32),
            pltpu.VMEM((tokens, PANEL), BF16),
            pltpu.VMEM((tokens, PANEL), BF16),
            pltpu.VMEM((tokens, n_quant), BF16),
            pltpu.VMEM((rows, PANEL), BF16),
            pltpu.VMEM((rows, PANEL), jnp.int32),
            pltpu.VMEM((2, n_feat, PANEL, width), F32),
            pltpu.VMEM((n_feat, PANEL, width), F32),
            pltpu.VMEM((n_feat, n_tok, strip, width), F32),
            pltpu.VMEM((n_tok, PANEL, PANEL), F32),
            pltpu.VMEM((PANEL, PANEL), F32),
            pltpu.VMEM((PANEL, PANEL), F32),
            pltpu.VMEM((PANEL, PANEL), F32),
            pltpu.VMEM((PANEL, PANEL), F32),
            dma((3,)), dma((n_chunks,)), dma((n_pieces,)),
            dma((n_pieces,)), dma((n_pieces,)), dma((n_pieces,)),
            dma((n_tok - 1,)), dma((n_tok - 1,)), dma((4,)), dma((2,)),
            dma((3, n_err)), dma((n_err,)),
            dma((n_feat, n_tok - 1)), dma((n_feat, n_tok - 1)),
            dma((n_feat, n_tok - 1)), dma((n_feat, n_tok - 1)),
            dma((n_feat, n_tok)), dma((n_feat, n_tok)),
        ],
        compiler_params=pltpu.CompilerParams(
            collective_id=0, has_side_effects=True, vmem_limit_bytes=32 * 1024 * 1024),
        name="exchange",
    )(*[pltpu.with_memory_space_constraint(x, pltpu.HBM)
        for x in (quantized, exponents.T, weights, keep_mask)])


def update_kernel(feat_ref, product_ref, error_ref, weights_ref, out_ref):
    error = error_ref[...]
    both = jnp.concatenate([error, error], axis=1)
    update = jnp.dot(both, product_ref[...], preferred_element_type=F32)
    out_ref[...] = (weights_ref[...].astype(F32) + update).astype(BF16)

    @pl.when(feat_ref[0] == 0)
    def _():
        out_ref[:, :PANEL] = weights_ref[:, :PANEL] - error


def apply_update(feat, product, error, weights, tile=512):
    rows, columns = weights.shape
    return pl.pallas_call(
        update_kernel,
        grid=(rows // tile,),
        out_shape=jax.ShapeDtypeStruct(weights.shape, BF16),
        in_specs=[
            pl.BlockSpec(memory_space=pltpu.SMEM),
            pl.BlockSpec(memory_space=pltpu.VMEM),
            pl.BlockSpec((tile, PANEL), lambda g: (g, 0)),
            pl.BlockSpec((tile, columns), lambda g: (g, 0)),
        ],
        out_specs=pl.BlockSpec((tile, columns), lambda g: (g, 0)),
        compiler_params=pltpu.CompilerParams(vmem_limit_bytes=24 * 1024 * 1024),
        name="update",
    )(feat, product, error, weights)


def shards(quantized, exponents, weights, keep_mask):
    product, error = exchange(quantized, exponents, weights, keep_mask)
    feat = lax.axis_index("feat").astype(jnp.int32).reshape(1)
    return apply_update(feat, product, error, weights)


def solution(mesh):
    placed = (
        P("tok", "feat"),
        P("tok", "feat"),
        P(("tok", "row"), "feat"),
        P(("tok", "row"), None),
    )
    return jax.shard_map(
        shards, mesh=mesh, in_specs=placed, out_specs=P(("tok", "row"), "feat"), check_vma=False
    )
```
